32 devices in a mesh: dev: 8 (over z, x), ma: 4 (over y, core).
Axes of the slice: x: 2, y: 2, z: 4, core: 2. Of those that a mesh axis runs over, the one named last changes fastest.
Arguments:
- inputs: bfloat16 [8192, 2048], P('ma', 'dev'), may hold values from -6 to 6
- cotangent: bfloat16 [8192, 2048], P('ma', 'dev'), may hold values from -6 to 6
- factors: bfloat16 [4, 64, 16384], P(None, 'ma', 'dev'), may hold values from -0.5 to 0.5
- exponents: int32 [4, 64], P(None, 'ma'), may hold values from -6 to -4
- error_buffer: bfloat16 [8, 4, 64, 16384], P('dev', None, 'ma'), may hold values from -96 to 96
Outputs:
- output: bfloat16 [8192, 2048], P('ma', 'dev')
- input_grad: bfloat16 [8192, 2048], P('ma', 'dev')
- grad_mean: float32 [4, 64, 16384], P(None, 'ma', 'dev')
- new_error: bfloat16 [8, 4, 64, 16384], P('dev', None, 'ma')
The draws below stay inside these ranges and needn't reach their ends.
All inputs are finite; a program needn't handle non-finite values.
Results may differ from the reference program's by a relative error of at most 0.0057.
Values may be sent and summed in bfloat16 or wider, within the bound.
A program may use at most 64 MiB of HBM per device.

```python
import jax
import jax.numpy as jnp
from jax import lax

NB = 64
B = 128
D = 8192
FACTORS = 4
TOK_DEV = 256
GROUPS = 8
TOKENS = 2048


def place_ends(entries, stream_key, low, top_value):
    shape = entries.shape
    index_at = [jax.random.randint(jax.random.fold_in(stream_key, axis), (), 0, shape[axis]) for axis in range(len(shape))]
    entries = entries.at[tuple(index_at)].set(low)
    longest = shape.index(max(shape))
    index_at[longest] = (index_at[longest] + 1) % shape[longest]
    return entries.at[tuple(index_at)].set(top_value)


def level_of(key, shape, shards, least, top_value):
    gain, own = 1.0, jax.random.fold_in(key, 6)
    for dim, shards_of in shards:
        steps = jnp.exp(jax.random.uniform(jax.random.fold_in(own, dim), (shards_of,), jnp.float32, least / len(shards), top_value / len(shards)))
        gain = gain * jnp.repeat(steps, shape[dim] // shards_of).reshape([-1 if axis == dim else 1 for axis in range(len(shape))])
    return gain


def gaussian(stream_key, extent, width, limit, shards=(), kind=jnp.bfloat16):
    array = width * jax.random.normal(stream_key, extent, jnp.float32)
    if shards:
        array = array * level_of(stream_key, extent, shards, -0.22, 0.18)
    return jnp.clip(array, -limit, limit).astype(kind)


def setup_inputs(seed: int = 0) -> dict:
    key_of = jax.random.split(jax.random.key(seed), 6)
    inputs = gaussian(key_of[0], (D, TOKENS), 1.0, 6.0, ((0, 4), (1, 8)))
    cotangent = gaussian(key_of[1], (D, TOKENS), 1.0, 6.0, ((0, 4), (1, 8)))
    factors = gaussian(key_of[2], (FACTORS, NB, B * B), B ** -0.5, 0.5, ((1, 4), (2, 8)))
    exponents = place_ends(jax.random.randint(key_of[3], (FACTORS, NB), -6, -3), jax.random.fold_in(key_of[3], 1), -6, (-3) - 1).astype(jnp.int32)
    error_buffer = gaussian(key_of[4], (GROUPS, FACTORS, NB, B * B), 16.0, 96.0, ((0, 8), (2, 4)))
    return {"inputs": inputs, "cotangent": cotangent, "factors": factors, "exponents": exponents, "error_buffer": error_buffer}


code_limit = 127.0

def permute(values):
    tok_count = values.shape[-1]
    grouped = values.reshape(NB, B // NB, NB, tok_count)
    return jnp.transpose(grouped, (2, 1, 0, 3)).reshape(NB, B, tok_count)

def block_forward(weights, values):
    return jnp.einsum('ncd,nct->ndt', weights.astype(jnp.float32), values.astype(jnp.float32))

def block_backward(weights, values):
    return jnp.einsum('ncd,ndt->nct', weights.astype(jnp.float32), values.astype(jnp.float32))

def outer_sum(left, right):
    return jnp.einsum('nct,ndt->ncd', left.astype(jnp.float32), right.astype(jnp.float32))

def reference(inputs, cotangent, factors, exponents, error_buffer):
    matrices = factors.reshape(FACTORS, NB, B, B)
    scale_inverse = jnp.left_shift(jnp.ones_like(exponents), -exponents).astype(jnp.float32)[:, :, None]

    def split_groups(whole):
        return jnp.transpose(whole.reshape(NB, B, GROUPS, TOK_DEV), (2, 0, 1, 3))

    def join_groups(parts):
        return jnp.transpose(parts, (1, 2, 0, 3)).reshape(NB * B, GROUPS * TOK_DEV)

    def one_group(code_total, group_items):
        block_in, block_cot, error_part = group_items
        first_out = block_forward(matrices[0], block_in).astype(jnp.bfloat16)
        mixed_one = permute(first_out)
        second_out = block_forward(matrices[1], mixed_one).astype(jnp.bfloat16)
        pre_gelu = permute(second_out)
        hidden_wide, gelu_back = jax.vjp(jax.nn.gelu, pre_gelu.astype(jnp.float32))
        hidden = hidden_wide.astype(jnp.bfloat16)
        third_out = block_forward(matrices[2], hidden).astype(jnp.bfloat16)
        mixed_two = permute(third_out)
        fourth_out = block_forward(matrices[3], mixed_two).astype(jnp.bfloat16)
        output_part = (block_in.astype(jnp.float32) + permute(fourth_out).astype(jnp.float32)).astype(jnp.bfloat16)
        back_four = permute(block_cot)
        d_mixed_two = block_backward(matrices[3], back_four).astype(jnp.bfloat16)
        d_third = permute(d_mixed_two)
        d_pre = gelu_back(block_backward(matrices[2], d_third))[0].astype(jnp.bfloat16)
        d_second = permute(d_pre)
        d_mixed_one = block_backward(matrices[1], d_second).astype(jnp.bfloat16)
        d_first = permute(d_mixed_one)
        grad_part = (block_cot.astype(jnp.float32) + block_backward(matrices[0], d_first)).astype(jnp.bfloat16)
        gradients = jnp.stack([outer_sum(block_in, d_first), outer_sum(mixed_one, d_second), outer_sum(hidden, d_third), outer_sum(mixed_two, back_four)]).reshape(FACTORS, NB, B * B)
        totals = gradients + error_part.astype(jnp.float32)
        code_values = jnp.clip(totals * scale_inverse, -code_limit, code_limit)
        new_part = (totals - code_values / scale_inverse).astype(jnp.bfloat16)
        return (code_total + code_values, (output_part, grad_part, new_part))
    code_total, stacked = lax.scan(one_group, jnp.zeros((FACTORS, NB, B * B), jnp.float32), (split_groups(inputs), split_groups(cotangent), error_buffer))
    grad_mean = code_total / scale_inverse / GROUPS
    return (join_groups(stacked[0]), join_groups(stacked[1]), grad_mean, stacked[2])
```

```python
import functools

import jax
import jax.numpy as jnp
from jax import lax
from jax.experimental import pallas as pl
from jax.experimental.pallas import tpu as pltpu
from jax.sharding import PartitionSpec as P

B = 128
LANES = 128
PAD = 8
Q = 4
LIMIT = 127.0
C0 = 0.7978845608028654
C1 = 0.044715
F32 = jnp.float32
BF16 = jnp.bfloat16
MESH = pl.DeviceIdType.MESH
COT, ONE = range(2)
HID, D3, M2, D2, B4, M1, D1, LAST = range(8)


def dot(a, b):
    return lax.dot_general(a, b, (((1,), (0,)), ((), ())), preferred_element_type=F32)


def dot_nt(a, b):
    return lax.dot_general(a, b, (((1,), (1,)), ((), ())), preferred_element_type=F32)


def kernel(
    G, M, inp, cot, fac, expo, err, out, igrad, gmean, nerr,
    x_v, c_v, e_v, gs, tx, rx, sf1, sf2, sb3, sl, op, ox, od, wg0, wg, wn0, wt0, wn1, wn, wt, cod, crx, m_v,
    ld, st, xs, xr, ys, yr, ws, wr, ps, pr, ks, kr, os, orr, cs_s, cs_r, qs, qr,
):
    F, nb, S = fac.shape
    C = x_v.shape[0]
    Y = M // C
    NBT = M * nb
    U = B // NBT
    CS = S // B
    SB = C * nb
    PITCH = B + PAD
    SLP = U * SB + PAD
    JR = NBT * U // Q
    ma = lax.axis_index("ma")
    dev = lax.axis_index("dev")
    y, c = ma // C, lax.rem(ma, C)
    s0 = y * SB
    half_group = G // 2
    partner = dev + 1 - 2 * lax.rem(dev, 2)

    def lanes(h):
        return slice(h * LANES, (h + 1) * LANES)

    def half(dc):
        return lax.rem(c + dc, C)

    def back(dc):
        return lax.rem(c + C - dc, C)

    def at(dy, dc):
        return {"ma": lax.rem(y + dy, Y) * C + lax.rem(c + dc, C)}

    def loop(lo, hi, fn, unroll=1):
        def one(i, _):
            fn(i)
            return 0

        lax.fori_loop(lo, hi, one, 0, unroll=unroll)

    loads = []
    for h in range(C):
        loads.append(pltpu.make_async_copy(cot.at[:, lanes(h)], c_v.at[h], ld.at[h]))
    for h in range(C):
        loads.append(pltpu.make_async_copy(inp.at[:, lanes(h)], x_v.at[h], ld.at[C + h]))
    loads.append(pltpu.make_async_copy(err.at[0], e_v, ld.at[2 * C]))
    own = [pltpu.make_async_copy(fac.at[0], wg0.at[dev], ld.at[2 * C + 1])]
    for f in range(1, F):
        own.append(pltpu.make_async_copy(fac.at[f], wg.at[f - 1, dev, c, y], ld.at[2 * C + 1 + f]))
    for cp in loads[:C]:
        cp.start()
    for cp in own:
        cp.start()
    for cp in loads[C:]:
        cp.start()

    barrier = pltpu.get_barrier_semaphore()
    for d in range(1, M):
        pl.semaphore_signal(barrier, inc=1, device_id={"ma": lax.rem(ma + d, M)}, device_id_type=MESH)

    def greet(d):
        pl.semaphore_signal(barrier, inc=1, device_id={"dev": lax.rem(dev + d, G)}, device_id_type=MESH)

    loop(1, G, greet)

    def remote(src, dst, send, recv, to):
        return pltpu.make_async_remote_copy(
            src_ref=src, dst_ref=dst, send_sem=send, recv_sem=recv, device_id=to, device_id_type=MESH
        )

    def slot_of(f, g):
        return wg0.at[g] if f == 0 else wg.at[f - 1, g, c]

    def y_copy(f, dy):
        return remote(
            fac.at[f], wg.at[f - 1, dev, c, y], ys.at[f, dy], yr.at[f, dy], at(dy, 0)
        )

    def w_copy(f, d):
        source = fac.at[0] if f == 0 else wg.at[f - 1, dev, c]
        return remote(source, slot_of(f, dev), ws.at[f, d], wr.at[f, d], {"dev": lax.rem(dev + 2 * d, G)})

    def p_copy(f, d, slot):
        return remote(slot_of(f, slot), slot_of(f, slot), ps.at[f, d], pr.at[f, d], {"dev": partner})

    def k_copy(f, dc, n, slot):
        return remote(
            wg.at[f - 1, slot, c], wg.at[f - 1, slot, c], ks.at[f, dc, n], kr.at[f, dc, n], at(0, dc)
        )

    def from_z(d):
        return lax.rem(dev + G - 2 * d, G)

    def from_x(d):
        return lax.rem(partner + G - 2 * d, G)

    def spread_on(f, n, slot):
        if f:
            for dc in range(1, C):
                k_copy(f, dc, n, slot).start()

    def forward(f):
        def one(d):
            w_copy(f, d).wait_recv()
            p_copy(f, d, from_z(d)).start()
            spread_on(f, d, from_z(d))

        loop(1, half_group, one)

    def gather(f):
        def one(d):
            p_copy(f, d, from_x(d)).wait_recv()
            spread_on(f, half_group + d, from_x(d))

        loop(0, half_group, one)

    def push(f):
        own[f].wait()
        if f:
            for dy in range(1, Y):
                y_copy(f, dy).wait_recv()
        loop(1, half_group, lambda d: w_copy(f, d).start())

    def pair(f):
        p_copy(f, 0, dev).start()
        spread_on(f, 0, dev)

    def x_copy(k, dy, dc, q):
        jq = lax.rem(lax.rem(y + dy, Y) * (Q // Y) + q, Q)
        rows = pl.ds(pl.multiple_of(jq * JR, JR), JR)
        return remote(
            tx.at[k, dc, rows], rx.at[k, rows, pl.ds(pl.multiple_of(ma * nb, nb), nb), :],
            xs.at[k, dy * C + dc, q], xr.at[k, dy * C + dc, q], at(dy, dc),
        )

    def chunk(q):
        return lax.rem(y * (Q // Y) + q, Q)

    def arrive(k, q):
        for dy in range(Y):
            for dc in range(C):
                if dy or dc:
                    x_copy(k, dy, dc, q).wait_recv()

    def launch(k, dc, qs_):
        for q in qs_:
            for dy in range(1, Y):
                x_copy(k, dy, dc, q).start()

    def near(k, dc):
        if dc:
            for q in range(Q):
                x_copy(k, 0, dc, q).start()

    def o_copy(k, dc):
        blocks = half(dc) * nb
        if k < B4:
            src = op.at[k, pl.ds(pl.multiple_of(blocks * B, B), nb * B), :]
        elif k < D1:
            src = rx.at[COT if k == B4 else ONE, pl.ds(pl.multiple_of((s0 + blocks) * U, U), nb * U)]
        else:
            src = od.at[k - D1, dc]
        dst = ox.at[k, dc - 1]
        if B4 <= k < D1:
            dst = dst.reshape(nb * U, NBT, LANES)
        return remote(src, dst, os.at[k, dc], orr.at[k, dc], at(0, dc))

    def swap(k):
        for dc in range(1, C):
            o_copy(k, dc).start()

    def swapped(k):
        for dc in range(1, C):
            o_copy(k, dc).wait_recv()

    def q_copy(f, d):
        return remote(cod.at[f, d], crx.at[f, half_group + d], qs.at[f, d], qr.at[f, d], {"dev": partner})

    def c_copy(f, d):
        return remote(
            cod.at[f, half_group + d], crx.at[f, d], cs_s.at[f, d], cs_r.at[f, d], {"dev": lax.rem(dev + 2 * d, G)}
        )

    def combine(f):
        def one(d):
            q_copy(f, d).wait_recv()
            both = cod[f, half_group + d].astype(F32) + crx[f, half_group + d].astype(F32)
            cod[f, half_group + d] = both.astype(BF16)
            c_copy(f, d).start()

        loop(1, half_group, one)
        q_copy(f, 0).wait_recv()
        crx[f, 0] = (cod[f, half_group].astype(F32) + crx[f, half_group].astype(F32)).astype(BF16)

    def scatter(i, value):
        for u in range(U):
            gs[pl.ds(u * nb + i, NBT, stride=U * nb), :] = value[u * NBT:(u + 1) * NBT]

    def pack(k, dc):
        def one(q):
            rows = gs[pl.ds(pl.multiple_of(q * JR * nb, JR * nb), JR * nb), :]
            value = rows.astype(BF16).reshape(JR, nb, LANES)
            to = pl.ds(pl.multiple_of(q * JR, JR), JR)
            tx[k, dc, to] = value
            if dc == 0:
                rx[k, to, pl.ds(pl.multiple_of(ma * nb, nb), nb), :] = value

        loop(0, Q, one)

    def rows_at(n):
        return pl.ds(pl.multiple_of(n * B, B), B)

    def block(k, j):
        return rx[k, pl.ds(j * U, U)].reshape(B, LANES)

    def gathered(ref, i, pitch, step):
        return jnp.concatenate([ref[pl.ds(u * step + i, NBT, stride=pitch), :] for u in range(U)], axis=0)

    def stored(ref, j, value):
        ref[pl.ds(pl.multiple_of(j * PITCH, 8), B), :] = value

    def kept(k, p, value):
        beyond = (p // SB + Y - 1) // Y
        op[k, rows_at(p - beyond * (p - SB)), :] = value

    def widen(piece):
        def one(g):
            for s in range(CS):
                to = pl.multiple_of((g * CS + s) * nb, nb)
                gs[pl.ds(to, nb), :] = piece(g, s)

        loop(0, G, one)

    def weights_first():
        widen(lambda g, s: wg0[g, :, s * B:(s + 1) * B].astype(F32))

        def take(n):
            w = gs[pl.ds(n, B, stride=nb), :]
            wn0[n] = w.astype(BF16)
            wt0[n] = w.T.astype(BF16)

        loop(0, nb, take, 2)

    def weights(f):
        for dc in range(1, C):
            def came(n, dc=dc):
                k_copy(f, dc, n, dev).wait_recv()

            loop(0, G, came)

        def group(m):
            yy, cc = m // C, lax.rem(m, C)
            widen(lambda g, s: wg[f - 1, g, cc, yy, :, s * B:(s + 1) * B].astype(F32))

            def take(n):
                j = m * nb + n
                w = gs[pl.ds(n, B, stride=nb), :]
                if f == 1:
                    for u in range(U):
                        side = gs[pl.ds((u * NBT + s0) * nb + n, SB, stride=nb), :]
                        wn1[j, u * SB:(u + 1) * SB, :] = side.astype(BF16)
                else:
                    wn[f - 2, j] = w.astype(BF16)
                wt[f - 1, j] = w.T.astype(BF16)

            loop(0, nb, take, 2)

        loop(0, M, group)

    def gradient(f, left, right):
        def one(n):
            a = jnp.concatenate([left(dc, n) for dc in range(C)], axis=1)
            b = jnp.concatenate([right(dc, n) for dc in range(C)], axis=1)
            gs[pl.ds(n, B, stride=nb), :] = dot_nt(a, b)

        loop(0, nb, one, 4)
        row = lax.broadcasted_iota(jnp.int32, (nb, B), 0)
        power = jnp.zeros((nb, B), jnp.int32)
        for n in range(nb):
            power = jnp.where(row == n, expo[f, n], power)
        scale = jnp.left_shift(jnp.ones_like(power), -power).astype(F32)
        inverse = jnp.left_shift(jnp.ones_like(power), 24 + power).astype(F32) * (2.0 ** -24)

        def quantize(g, slot):
            for s in range(CS):
                col = pl.ds(pl.multiple_of((g * CS + s) * B, B), B)
                total = gs[pl.ds(pl.multiple_of((g * CS + s) * nb, nb), nb), :] + e_v[f, :, col].astype(F32)
                code = jnp.clip(total * scale, -LIMIT, LIMIT)
                e_v[f, :, col] = (total - code * inverse).astype(BF16)
                cod[f, slot, :, s * B:(s + 1) * B] = code.astype(BF16)

        def away(step):
            d = lax.rem(step + 1, half_group)
            quantize(lax.rem(partner + 2 * d, G), d)
            q_copy(f, d).start()

        loop(0, half_group, away)
        loop(0, half_group, lambda d: quantize(lax.rem(dev + 2 * d, G), half_group + d))
        pltpu.make_async_copy(e_v.at[f], nerr.at[0, f], st.at[f]).start()
        return inverse

    def op_rows(k, dc, n):
        if dc:
            return ox[k, dc - 1, rows_at(n), :]
        if k < B4:
            return op[k, rows_at(c * nb + n), :]
        if k < D1:
            return block(COT if k == B4 else ONE, ma * nb + n)
        return od[k - D1, 0, rows_at(n), :]

    def ops(k):
        return functools.partial(op_rows, k)

    def spread_cot(dc):
        loop(0, nb, lambda i: scatter(i, c_v[half(dc), rows_at(i), :].astype(F32)), 4)
        pack(COT, dc)

    for h in range(C):
        loads[h].wait()
    spread_cot(C - 1)
    pl.semaphore_wait(barrier, M - 1 + G - 1)
    push(0)
    pair(0)
    for f in range(1, F):
        for dy in range(1, Y):
            y_copy(f, dy).start()
    early, late = tuple(range(Q // Y)), tuple(range(Q // Y, Q))
    launch(COT, C - 1, early)
    near(COT, C - 1)
    for dc in range(C - 2, -1, -1):
        spread_cot(dc)
        launch(COT, dc, early)
        near(COT, dc)

    forward(0)
    push(1)
    gather(0)
    pair(1)
    weights_first()
    for h in range(C):
        loads[C + h].wait()
    for dc in range(C - 1, -1, -1):
        loop(0, nb, lambda i: scatter(i, dot(wt0[i], x_v[half(dc), rows_at(i), :])), 4)
        pack(ONE, dc)
        launch(ONE, dc, range(Q))
        near(ONE, dc)
    forward(1)
    push(2)
    gather(1)
    pair(2)
    weights(1)
    forward(2)
    push(3)
    gather(2)
    pair(3)
    weights(2)

    def first(q):
        arrive(ONE, q)
        base = chunk(q) * (NBT // Q)
        loop(0, NBT // Q, lambda n: stored(sf1, base + n, dot(wt[0, base + n], block(ONE, base + n))), 4)

    for q in early:
        first(q)
    swap(M1)
    for q in late[:-1]:
        first(q)
    for dc in range(C - 1, -1, -1):
        launch(COT, dc, late)
    for q in late[-1:]:
        first(q)
    forward(3)

    def middle(p):
        i = lax.rem(s0 + p, NBT)
        v = gathered(sf1, i, PITCH, NBT).astype(BF16).astype(F32)
        square = v * v
        t = jnp.tanh(C0 * (v + C1 * (square * v)))
        halved = 0.5 * (1.0 + t)
        hidden = (v * halved).astype(BF16)
        slope = halved + 0.5 * v * (1.0 - t * t) * (C0 * (1.0 + 3.0 * C1 * square))
        for u in range(U):
            sf1[pl.ds(u * NBT + i, NBT, stride=PITCH), :] = slope[u * NBT:(u + 1) * NBT]
        kept(HID, p, hidden)
        stored(sf2, i, dot(wt[1, i], hidden))

    loop(0, NBT, middle, 2)
    swap(HID)
    gather(3)
    weights(3)

    def side_rows(ref, f, j):
        return jnp.concatenate(
            [ref[f, j, pl.ds(pl.multiple_of(u * NBT + s0, nb), SB), :] for u in range(U)], axis=0
        )

    def fourth(p):
        j = lax.rem(s0 + p, NBT)
        two = gathered(sf2, j, PITCH, NBT).astype(BF16)
        kept(M2, p, two)
        sl[pl.ds(pl.multiple_of(j * SLP, 8), U * SB), :] = dot(side_rows(wt, F - 2, j), two)

    loop(0, NBT, fourth, 4)
    swap(M2)

    def collect(k):
        for dc in range(C - 1, -1, -1):
            def one(n, dc=dc):
                value = gathered(sl, half(dc) * nb + n, SLP, SB)
                od[k - D1, dc, rows_at(n), :] = value.astype(BF16)

            loop(0, nb, one, 4)
            if dc:
                o_copy(k, dc).start()

    collect(LAST)

    def third_back(q):
        base = chunk(q) * (NBT // Q)
        loop(0, NBT // Q, lambda n: stored(sb3, base + n, dot(wn[1, base + n], block(COT, base + n))), 4)

    for q in early:
        arrive(COT, q)
    swap(B4)
    for q in early:
        third_back(q)
    loads[2 * C].wait()
    inverses = {}
    swapped(M2)
    swapped(B4)
    inverses[3] = gradient(3, ops(M2), ops(B4))
    for q in late:
        arrive(COT, q)
        third_back(q)

    def second_back(p):
        i = lax.rem(s0 + p, NBT)
        d_third = gathered(sb3, i, PITCH, NBT).astype(BF16)
        kept(D3, p, d_third)
        slope = gathered(sf1, i, PITCH, NBT)
        stored(sf2, i, dot(wn[0, i], d_third) * slope)

    loop(0, NBT, second_back, 4)
    swap(D3)
    combine(3)

    def first_back(p):
        j = lax.rem(s0 + p, NBT)
        d_second = gathered(sf2, j, PITCH, NBT).astype(BF16)
        kept(D2, p, d_second)
        sl[pl.ds(pl.multiple_of(j * SLP, 8), U * SB), :] = dot(wn1[j], d_second)

    loop(0, NBT, first_back, 4)
    swap(D2)
    collect(D1)
    swapped(HID)
    swapped(D3)
    inverses[2] = gradient(2, ops(HID), ops(D3))
    swapped(M1)
    swapped(D2)
    inverses[1] = gradient(1, ops(M1), ops(D2))
    combine(2)
    swapped(D1)
    inverses[0] = gradient(0, lambda dc, n: x_v[back(dc), rows_at(n), :], ops(D1))
    combine(1)
    stores = []

    def save(ref, value_ref, h, sem):
        to = pl.ds(pl.multiple_of(h * LANES, LANES), LANES)
        stores.append(pltpu.make_async_copy(value_ref, ref.at[:, to], sem))
        stores[-1].start()

    for dc in range(C):
        def last_back(n, dc=dc):
            h = back(dc)
            value = c_v[h, rows_at(n), :].astype(F32) + dot(wn0[n], op_rows(D1, dc, n))
            c_v[h, rows_at(n), :] = value.astype(BF16)

        loop(0, nb, last_back, 4)
        save(igrad, c_v.at[back(dc)], back(dc), st.at[2 * F + dc])
    combine(0)

    def mean(f):
        loop(1, half_group, lambda d: c_copy(f, d).wait_recv())

        def column(s):
            col = pl.ds(pl.multiple_of(s * B, B), B)
            total = crx[f, 0, :, col].astype(F32)
            for g in range(1, half_group):
                total = total + crx[f, g, :, col].astype(F32)
            m_v[f, :, col] = total * inverses[f] / G

        loop(0, CS, column)
        stores.append(pltpu.make_async_copy(m_v.at[f], gmean.at[f], st.at[F + f]))
        stores[-1].start()

    swapped(LAST)
    for dc in range(C):
        ref = ox.at[LAST, dc - 1] if dc else od.at[LAST - D1, 0]

        def finish(n, dc=dc, ref=ref):
            value = x_v[back(dc), rows_at(n), :].astype(F32) + ref[rows_at(n), :].astype(F32)
            ref[rows_at(n), :] = value.astype(BF16)

        loop(0, nb, finish, 4)
        save(out, ref, back(dc), st.at[2 * F + C + dc])
    for f in (3, 2, 1, 0):
        mean(f)
    for f in range(F):
        pltpu.make_async_copy(e_v.at[f], nerr.at[0, f], st.at[f]).wait()
    for cp in stores:
        cp.wait()

    def handed(d):
        for f in range(F):
            w_copy(f, d).wait_send()
            q_copy(f, d).wait_send()
            c_copy(f, d).wait_send()
            p_copy(f, d, from_z(d)).wait_send()

    loop(1, half_group, handed)
    for f in range(F):
        p_copy(f, 0, dev).wait_send()
        q_copy(f, 0).wait_send()
    for f in range(1, F):
        for dy in range(1, Y):
            y_copy(f, dy).wait_send()
        for dc in range(1, C):
            loop(0, G, lambda n: k_copy(f, dc, n, dev).wait_send())
    for k in range(8):
        for dc in range(1, C):
            o_copy(k, dc).wait_send()
    for k in (COT, ONE):
        for dy in range(Y):
            for dc in range(C):
                if dy or dc:
                    for q in range(Q):
                        x_copy(k, dy, dc, q).wait_send()


def step(G, M, inp, cot, fac, expo, err):
    F, nb, S = fac.shape
    R, T = inp.shape
    C = T // LANES
    Y = M // C
    NBT = M * nb
    U = B // NBT
    SB = C * nb
    hbm = pl.BlockSpec(memory_space=pl.ANY)
    dma = pltpu.SemaphoreType.DMA
    return pl.pallas_call(
        functools.partial(kernel, G, M),
        out_shape=(
            jax.ShapeDtypeStruct((R, T), BF16),
            jax.ShapeDtypeStruct((R, T), BF16),
            jax.ShapeDtypeStruct(fac.shape, F32),
            jax.ShapeDtypeStruct(err.shape, BF16),
        ),
        in_specs=[hbm, hbm, hbm, pl.BlockSpec(memory_space=pltpu.SMEM), hbm],
        out_specs=(hbm,) * 4,
        scratch_shapes=[
            pltpu.VMEM((C, R, LANES), BF16),
            pltpu.VMEM((C, R, LANES), BF16),
            pltpu.VMEM((F, nb, B * B), BF16),
            pltpu.VMEM((R, LANES), F32),
            pltpu.VMEM((2, C, NBT * U, nb, LANES), BF16),
            pltpu.VMEM((2, NBT * U, NBT, LANES), BF16),
            pltpu.VMEM((NBT * (B + PAD), LANES), F32),
            pltpu.VMEM((NBT * (B + PAD), LANES), F32),
            pltpu.VMEM((NBT * (B + PAD), LANES), F32),
            pltpu.VMEM((NBT * (U * SB + PAD), LANES), F32),
            pltpu.VMEM((4, (SB + 1) * B, LANES), BF16),
            pltpu.VMEM((8, C - 1, R, LANES), BF16),
            pltpu.VMEM((2, C, R, LANES), BF16),
            pltpu.VMEM((G, nb, S), BF16),
            pltpu.VMEM((F - 1, G, C, Y, nb, S), BF16),
            pltpu.VMEM((nb, B, B), BF16),
            pltpu.VMEM((nb, B, B), BF16),
            pltpu.VMEM((NBT, U * SB, B), BF16),
            pltpu.VMEM((F - 2, NBT, B, B), BF16),
            pltpu.VMEM((F - 1, NBT, B, B), BF16),
            pltpu.VMEM((F, G, nb, S), BF16),
            pltpu.VMEM((F, G, nb, S), BF16),
            pltpu.VMEM((F, nb, S), F32),
            dma((2 * C + 1 + F,)),
            dma((2 * F + 2 * C,)),
            dma((2, M, Q)),
            dma((2, M, Q)),
            dma((F, Y)),
            dma((F, Y)),
            dma((F, G // 2)),
            dma((F, G // 2)),
            dma((F, G // 2)),
            dma((F, G // 2)),
            dma((F, C, G)),
            dma((F, C, G)),
            dma((8, C)),
            dma((8, C)),
            dma((F, G // 2)),
            dma((F, G // 2)),
            dma((F, G // 2)),
            dma((F, G // 2)),
        ],
        compiler_params=pltpu.CompilerParams(
            collective_id=0, has_side_effects=True, vmem_limit_bytes=62 * 1024 * 1024
        ),
    )(inp, cot, fac, expo, err)


def solution(mesh):
    G, M = mesh.shape["dev"], mesh.shape["ma"]
    in_specs = (
        P("ma", "dev"),
        P("ma", "dev"),
        P(None, "ma", "dev"),
        P(None, "ma"),
        P("dev", None, "ma", None),
    )
    out_specs = (P("ma", "dev"), P("ma", "dev"), P(None, "ma", "dev"), P("dev", None, "ma", None))
    return jax.shard_map(
        functools.partial(step, G, M), mesh=mesh, in_specs=in_specs, out_specs=out_specs, check_vma=False
    )
```

```python
import functools

import jax
import jax.numpy as jnp
from jax import lax
from jax.experimental import pallas as pl
from jax.experimental.pallas import tpu as pltpu
from jax.sharding import PartitionSpec as P

B = 128
LANES = 128
PAD = 8
Q = 4
LIMIT = 127.0
C0 = 0.7978845608028654
C1 = 0.044715
F32 = jnp.float32
BF16 = jnp.bfloat16
MESH = pl.DeviceIdType.MESH
COT, ONE = range(2)
HID, D3, M2, D2, B4, M1, D1, LAST = range(8)


def dot(a, b):
    return lax.dot_general(a, b, (((1,), (0,)), ((), ())), preferred_element_type=F32)


def dot_nt(a, b):
    return lax.dot_general(a, b, (((1,), (1,)), ((), ())), preferred_element_type=F32)


def kernel(
    G, M, inp, cot, fac, expo, err, out, igrad, gmean, nerr,
    x_v, c_v, e_v, gs, tx, rx, sf1, sf2, sb3, slp, sl, op, ox, od, fv, wg0, wg, wn0, wt0, wn, wt, cod, crx, m_v,
    ld, st, xs, xr, ys, yr, ws, wr, ps, pr, ks, kr, os, orr, cs_s, cs_r, qs, qr,
):
    F, nb, S = fac.shape
    C = x_v.shape[0]
    Y = M // C
    NBT = M * nb
    U = B // NBT
    CS = S // B
    SB = C * nb
    PITCH = B + PAD
    SLP = U * SB + PAD
    XP = U * nb + PAD
    GP = nb + PAD
    JR = NBT * U // Q
    tiled = CS % 16 == 0
    ma = lax.axis_index("ma")
    dev = lax.axis_index("dev")
    y, c = ma // C, lax.rem(ma, C)
    s0 = y * SB
    sb2 = sf1 if tiled else sf2
    half_group = G // 2
    partner = dev + 1 - 2 * lax.rem(dev, 2)

    def lanes(h):
        return slice(h * LANES, (h + 1) * LANES)

    def half(dc):
        return lax.rem(c + dc, C)

    def back(dc):
        return lax.rem(c + C - dc, C)

    def at(dy, dc):
        return {"ma": lax.rem(y + dy, Y) * C + lax.rem(c + dc, C)}

    def loop(lo, hi, fn, unroll=1):
        def one(i, _):
            fn(i)
            return 0

        lax.fori_loop(lo, hi, one, 0, unroll=unroll)

    loads = []
    for h in range(C):
        loads.append(pltpu.make_async_copy(cot.at[:, lanes(h)], c_v.at[h], ld.at[h]))
    for h in range(C):
        loads.append(pltpu.make_async_copy(inp.at[:, lanes(h)], x_v.at[h], ld.at[C + h]))
    loads.append(pltpu.make_async_copy(err.at[0], e_v, ld.at[2 * C]))
    if tiled:
        own = [pltpu.make_async_copy(fac, fv, ld.at[2 * C + 1])]
    else:
        own = [pltpu.make_async_copy(fac.at[0], wg0.at[dev], ld.at[2 * C + 1])]
        for f in range(1, F):
            own.append(pltpu.make_async_copy(fac.at[f], wg.at[f - 1, dev, c, y], ld.at[2 * C + 1 + f]))
    for cp in own:
        cp.start()
    for cp in loads:
        cp.start()

    barrier = pltpu.get_barrier_semaphore()
    for d in range(1, M):
        pl.semaphore_signal(barrier, inc=1, device_id={"ma": lax.rem(ma + d, M)}, device_id_type=MESH)

    def greet(d):
        pl.semaphore_signal(barrier, inc=1, device_id={"dev": lax.rem(dev + d, G)}, device_id_type=MESH)

    loop(1, G, greet)

    def remote(src, dst, send, recv, to):
        return pltpu.make_async_remote_copy(
            src_ref=src, dst_ref=dst, send_sem=send, recv_sem=recv, device_id=to, device_id_type=MESH
        )

    def slot_of(f, g):
        if tiled:
            rows = pl.ds(pl.multiple_of(g * CS, CS), CS)
            return wn0.at[:, rows, :] if f == 0 else wn.at[f - 1, :, c, :, rows, :]
        return wg0.at[g] if f == 0 else wg.at[f - 1, g, c]

    def mine(f):
        if tiled:
            return wn.at[f - 1, y, c, :, pl.ds(pl.multiple_of(dev * CS, CS), CS), :]
        return wg.at[f - 1, dev, c, y]

    def y_copy(f, dy):
        return remote(mine(f), mine(f), ys.at[f, dy], yr.at[f, dy], at(dy, 0))

    def w_copy(f, d):
        return remote(slot_of(f, dev), slot_of(f, dev), ws.at[f, d], wr.at[f, d], {"dev": lax.rem(dev + 2 * d, G)})

    def p_copy(f, d, slot):
        return remote(slot_of(f, slot), slot_of(f, slot), ps.at[f, d], pr.at[f, d], {"dev": partner})

    def k_copy(f, dc, n, slot):
        return remote(slot_of(f, slot), slot_of(f, slot), ks.at[f, dc, n], kr.at[f, dc, n], at(0, dc))

    def from_z(d):
        return lax.rem(dev + G - 2 * d, G)

    def from_x(d):
        return lax.rem(partner + G - 2 * d, G)

    def spread_on(f, n, slot):
        if f:
            for dc in range(1, C):
                k_copy(f, dc, n, slot).start()

    def forward(f, lo=1, hi=None):
        def one(d):
            w_copy(f, d).wait_recv()
            p_copy(f, d, from_z(d)).start()
            spread_on(f, d, from_z(d))

        loop(lo, half_group if hi is None else hi, one)

    def gather(f):
        def one(d):
            p_copy(f, d, from_x(d)).wait_recv()
            spread_on(f, half_group + d, from_x(d))

        loop(0, half_group, one)

    def push(f):
        if f:
            for dy in range(1, Y):
                y_copy(f, dy).wait_recv()
        loop(1, half_group, lambda d: w_copy(f, d).start())

    def pair(f):
        p_copy(f, 0, dev).start()
        spread_on(f, 0, dev)

    def x_copy(k, dy, dc, q):
        jq = lax.rem(lax.rem(y + dy, Y) * (Q // Y) + q, Q)
        rows = pl.ds(pl.multiple_of(jq * JR, JR), JR)
        return remote(
            tx.at[k, dc, rows], rx.at[k, rows, pl.ds(pl.multiple_of(ma * nb, nb), nb), :],
            xs.at[k, dy * C + dc, q], xr.at[k, dy * C + dc, q], at(dy, dc),
        )

    def chunk(q):
        return lax.rem(y * (Q // Y) + q, Q)

    def arrive(k, q):
        for dy in range(Y):
            for dc in range(C):
                if dy or dc:
                    x_copy(k, dy, dc, q).wait_recv()

    def launch(k, dc, qs_):
        for q in qs_:
            for dy in range(1, Y):
                x_copy(k, dy, dc, q).start()

    def near(k, dc):
        if dc:
            for q in range(Q):
                x_copy(k, 0, dc, q).start()

    def o_copy(k, dc):
        blocks = half(dc) * nb
        if k < B4:
            src = op.at[k, pl.ds(pl.multiple_of(blocks * B, B), nb * B), :]
        elif k < D1:
            src = rx.at[COT if k == B4 else ONE, pl.ds(pl.multiple_of((s0 + blocks) * U, U), nb * U)]
        else:
            src = od.at[k - D1, dc]
        dst = ox.at[k, dc - 1]
        if B4 <= k < D1:
            dst = dst.reshape(nb * U, NBT, LANES)
        return remote(src, dst, os.at[k, dc], orr.at[k, dc], at(0, dc))

    def swap(k):
        for dc in range(1, C):
            o_copy(k, dc).start()

    def swapped(k):
        for dc in range(1, C):
            o_copy(k, dc).wait_recv()

    def q_copy(f, d):
        return remote(cod.at[f, d], crx.at[f, half_group + d], qs.at[f, d], qr.at[f, d], {"dev": partner})

    def c_copy(f, d):
        return remote(
            cod.at[f, half_group + d], crx.at[f, d], cs_s.at[f, d], cs_r.at[f, d], {"dev": lax.rem(dev + 2 * d, G)}
        )

    def combine(f):
        def one(d):
            q_copy(f, d).wait_recv()
            both = cod[f, half_group + d].astype(F32) + crx[f, half_group + d].astype(F32)
            cod[f, half_group + d] = both.astype(BF16)
            c_copy(f, d).start()

        loop(1, half_group, one)
        q_copy(f, 0).wait_recv()
        crx[f, 0] = (cod[f, half_group].astype(F32) + crx[f, half_group].astype(F32)).astype(BF16)

    def scatter(i, value):
        for u in range(U):
            gs[pl.ds(u * nb + i, NBT, stride=XP), :] = value[u * NBT:(u + 1) * NBT]

    def pack(k, dc):
        def one(j):
            rows = gs[pl.ds(pl.multiple_of(j * XP, 8), U * nb), :]
            value = rows.astype(BF16).reshape(U, nb, LANES)
            to = pl.ds(pl.multiple_of(j * U, U), U)
            tx[k, dc, to] = value
            if dc == 0:
                rx[k, to, pl.ds(pl.multiple_of(ma * nb, nb), nb), :] = value

        loop(0, NBT, one, 8)

    def rows_at(n):
        return pl.ds(pl.multiple_of(n * B, B), B)

    def block(k, j):
        return rx[k, pl.ds(j * U, U)].reshape(B, LANES)

    def gathered(ref, i, pitch, step):
        return jnp.concatenate([ref[pl.ds(u * step + i, NBT, stride=pitch), :] for u in range(U)], axis=0)

    def stored(ref, j, value):
        ref[pl.ds(pl.multiple_of(j * PITCH, 8), B), :] = value

    def take_side(k, ref):
        def one(p):
            op[k, rows_at(p), :] = gathered(ref, s0 + p, PITCH, NBT).astype(BF16)

        loop(0, SB, one, 8)

    def taken(k, ref, p, i, side):
        return op[k, rows_at(p), :] if side else gathered(ref, i, PITCH, NBT).astype(BF16)

    def widen(piece):
        def one(g):
            for s in range(CS):
                to = pl.multiple_of((g * CS + s) * GP, 8)
                gs[pl.ds(to, nb), :] = piece(g, s)

        loop(0, G, one)

    def arrange():
        for cp in own:
            cp.wait()
        if tiled:
            for f in range(F):
                for s in range(CS):
                    gs[(f * CS + s) * GP:(f * CS + s) * GP + nb, :] = fv[f, :, s * B:(s + 1) * B].astype(F32)
            for f in range(F):
                def one(n, f=f):
                    tile = gs[pl.ds(f * CS * GP + n, CS, stride=GP), :].astype(BF16)
                    rows = pl.ds(pl.multiple_of(dev * CS, CS), CS)
                    if f:
                        wn[f - 1, y, c, n, rows, :] = tile
                    else:
                        wn0[n, rows, :] = tile

                loop(0, nb, one, 4)

    def weights_first():
        if not tiled:
            widen(lambda g, s: wg0[g, :, s * B:(s + 1) * B].astype(F32))

        def take(n):
            if not tiled:
                wn0[n] = gs[pl.ds(n, B, stride=GP), :].astype(BF16)
            wt0[n] = wn0[n].T

        loop(0, nb, take, 8)

    def landed(f):
        for dc in range(1, C):
            def came(n, dc=dc):
                k_copy(f, dc, n, dev).wait_recv()

            loop(0, G, came)

    def flip(f):
        def group(m):
            yy, cc = m // C, lax.rem(m, C)
            if not tiled:
                widen(lambda g, s: wg[f - 1, g, cc, yy, :, s * B:(s + 1) * B].astype(F32))

            def take(n):
                if not tiled:
                    wn[f - 1, yy, cc, n] = gs[pl.ds(n, B, stride=GP), :].astype(BF16)
                wt[f - 1, yy, cc, n] = wn[f - 1, yy, cc, n].T

            loop(0, nb, take, 8)

        loop(0, M, group)

    def weights(f):
        landed(f)
        flip(f)

    def weight(ref, f, j):
        return ref[f - 1, j // SB, lax.rem(j, SB) // nb, lax.rem(j, nb)]

    def side_weight(ref, f, j):
        at_j = ref.at[f - 1, j // SB, lax.rem(j, SB) // nb, lax.rem(j, nb)]
        rows = [at_j[pl.ds(pl.multiple_of(u * NBT + s0, nb), SB), :] for u in range(U)]
        return jnp.concatenate(rows, axis=0)

    def gradient(f, left, right):
        def one(n):
            a = jnp.concatenate([left(dc, n) for dc in range(C)], axis=1)
            b = jnp.concatenate([right(dc, n) for dc in range(C)], axis=1)
            gs[pl.ds(n, B, stride=GP), :] = dot_nt(a, b)

        loop(0, nb, one, 8)
        row = lax.broadcasted_iota(jnp.int32, (nb, B), 0)
        power = jnp.zeros((nb, B), jnp.int32)
        for n in range(nb):
            power = jnp.where(row == n, expo[f, n], power)
        scale = jnp.left_shift(jnp.ones_like(power), -power).astype(F32)
        inverse = jnp.left_shift(jnp.ones_like(power), 24 + power).astype(F32) * (2.0 ** -24)

        def quantize(g, slot):
            for s in range(CS):
                col = pl.ds(pl.multiple_of((g * CS + s) * B, B), B)
                total = gs[pl.ds(pl.multiple_of((g * CS + s) * GP, 8), nb), :] + e_v[f, :, col].astype(F32)
                code = jnp.clip(total * scale, -LIMIT, LIMIT)
                e_v[f, :, col] = (total - code * inverse).astype(BF16)
                cod[f, slot, :, s * B:(s + 1) * B] = code.astype(BF16)

        def away(step):
            d = lax.rem(step + 1, half_group)
            quantize(lax.rem(partner + 2 * d, G), d)
            q_copy(f, d).start()

        loop(0, half_group, away)
        loop(0, half_group, lambda d: quantize(lax.rem(dev + 2 * d, G), half_group + d))
        pltpu.make_async_copy(e_v.at[f], nerr.at[0, f], st.at[f]).start()
        return inverse

    def op_rows(k, dc, n):
        if dc:
            return ox[k, dc - 1, rows_at(n), :]
        if k < B4:
            return op[k, rows_at(c * nb + n), :]
        if k < D1:
            return block(COT if k == B4 else ONE, ma * nb + n)
        return od[k - D1, 0, rows_at(n), :]

    def ops(k):
        return functools.partial(op_rows, k)

    def spread_cot(dc):
        loop(0, nb, lambda i: scatter(i, c_v[half(dc), rows_at(i), :].astype(F32)), 8)
        pack(COT, dc)

    early, late = tuple(range(Q // Y)), tuple(range(Q // Y, Q))
    arrange()
    pl.semaphore_wait(barrier, M - 1 + G - 1)
    push(0)
    pair(0)
    for f in range(1, F):
        for dy in range(1, Y):
            y_copy(f, dy).start()
    for h in range(C):
        loads[h].wait()
    for dc in range(C - 1, -1, -1):
        spread_cot(dc)
        launch(COT, dc, early)
        near(COT, dc)

    forward(0)
    push(1)
    pair(1)
    push(2)
    push(3)
    gather(0)
    weights_first()
    for h in range(C):
        loads[C + h].wait()
    for dc in range(C - 1, -1, -1):
        loop(0, nb, lambda i: scatter(i, dot(wt0[i], x_v[half(dc), rows_at(i), :])), 8)
        pack(ONE, dc)
        launch(ONE, dc, range(Q))
        near(ONE, dc)
    for dc in range(C - 1, -1, -1):
        launch(COT, dc, late)
    forward(1, 1, 2)
    pair(2)
    forward(1, 2)
    gather(1)
    weights(1)
    for q in early:
        arrive(COT, q)
    swap(B4)

    def first(q):
        arrive(ONE, q)
        base = chunk(q) * (NBT // Q)
        loop(0, NBT // Q, lambda n: stored(sf1, base + n, dot(weight(wt, 1, base + n), block(ONE, base + n))), 8)

    first(0)
    forward(2, 1, 2)
    pair(3)
    forward(2, 2)
    gather(2)
    weights(2)
    for q in early[1:]:
        first(q)
    swap(M1)
    for q in late[:-1]:
        first(q)
    forward(3, 1, 2)
    for q in late[-1:]:
        first(q)
    forward(3, 2, half_group - 1)

    def middle(p, side):
        i = lax.rem(s0 + p, NBT)
        v = gathered(sf1, i, PITCH, NBT).astype(BF16).astype(F32)
        square = v * v
        t = jnp.tanh(C0 * (v + C1 * (square * v)))
        halved = 0.5 * (1.0 + t)
        hidden = (v * halved).astype(BF16)
        slope = halved + 0.5 * v * (1.0 - t * t) * (C0 * (1.0 + 3.0 * C1 * square))
        if tiled:
            stored(slp, i, slope)
        else:
            for u in range(U):
                sf1[pl.ds(u * NBT + i, NBT, stride=PITCH), :] = slope[u * NBT:(u + 1) * NBT]
        if side:
            op[HID, rows_at(p), :] = hidden
        stored(sf2, i, dot(weight(wt, 2, i), hidden))

    loop(0, SB, lambda p: middle(p, True), 8)
    swap(HID)
    forward(3, half_group - 1)
    loop(SB, NBT, lambda p: middle(p, False), 8)
    take_side(M2, sf2)
    swap(M2)
    loads[2 * C].wait()
    inverses = {}
    swapped(M2)
    swapped(B4)
    inverses[3] = gradient(3, ops(M2), ops(B4))
    gather(3)
    landed(3)

    def collect(k):
        for dc in range(C - 1, -1, -1):
            def one(n, dc=dc):
                value = gathered(sl, half(dc) * nb + n, SLP, SB)
                od[k - D1, dc, rows_at(n), :] = value.astype(BF16)

            loop(0, nb, one, 8)
            if dc:
                o_copy(k, dc).start()

    def fourth(p, side):
        j = lax.rem(s0 + p, NBT)
        two = taken(M2, sf2, p, j, side)
        sl[pl.ds(pl.multiple_of(j * SLP, 8), U * SB), :] = dot(side_weight(wt, 3, j), two)

    def last_forward():
        flip(3)
        loop(0, SB, lambda p: fourth(p, True), 8)
        loop(SB, NBT, lambda p: fourth(p, False), 8)
        collect(LAST)

    if not tiled:
        last_forward()

    def third_back(q):
        base = chunk(q) * (NBT // Q)
        loop(0, NBT // Q, lambda n: stored(sb3, base + n, dot(weight(wn, 3, base + n), block(COT, base + n))), 8)

    for q in early:
        third_back(q)
    for q in late:
        arrive(COT, q)
        third_back(q)
    take_side(D3, sb3)
    swap(D3)
    combine(3)

    def second_back(p, side):
        i = lax.rem(s0 + p, NBT)
        slope = slp[pl.ds(pl.multiple_of(i * PITCH, 8), B), :] if tiled else gathered(sf1, i, PITCH, NBT)
        stored(sb2, i, dot(weight(wn, 2, i), taken(D3, sb3, p, i, side)) * slope)

    loop(0, SB, lambda p: second_back(p, True), 8)
    swapped(HID)
    swapped(D3)
    inverses[2] = gradient(2, ops(HID), ops(D3))
    loop(SB, NBT, lambda p: second_back(p, False), 8)
    take_side(D2, sb2)
    swap(D2)

    def first_back(p, side):
        j = lax.rem(s0 + p, NBT)
        sl[pl.ds(pl.multiple_of(j * SLP, 8), U * SB), :] = dot(side_weight(wn, 1, j), taken(D2, sb2, p, j, side))

    loop(0, SB, lambda p: first_back(p, True), 8)
    swapped(M1)
    swapped(D2)
    inverses[1] = gradient(1, ops(M1), ops(D2))
    loop(SB, NBT, lambda p: first_back(p, False), 8)
    collect(D1)
    combine(2)
    swapped(D1)
    inverses[0] = gradient(0, lambda dc, n: x_v[back(dc), rows_at(n), :], ops(D1))
    if tiled:
        last_forward()
    combine(1)
    stores = []

    def save(ref, value_ref, h, sem):
        to = pl.ds(pl.multiple_of(h * LANES, LANES), LANES)
        stores.append(pltpu.make_async_copy(value_ref, ref.at[:, to], sem))
        stores[-1].start()

    for dc in range(C):
        def last_back(n, dc=dc):
            h = back(dc)
            value = c_v[h, rows_at(n), :].astype(F32) + dot(wn0[n], op_rows(D1, dc, n))
            c_v[h, rows_at(n), :] = value.astype(BF16)

        loop(0, nb, last_back, 8)
        save(igrad, c_v.at[back(dc)], back(dc), st.at[2 * F + dc])
    combine(0)

    def mean(f):
        loop(1, half_group, lambda d: c_copy(f, d).wait_recv())

        def column(s):
            col = pl.ds(pl.multiple_of(s * B, B), B)
            total = crx[f, 0, :, col].astype(F32)
            for g in range(1, half_group):
                total = total + crx[f, g, :, col].astype(F32)
            m_v[f, :, col] = total * inverses[f] / G

        loop(0, CS, column)
        stores.append(pltpu.make_async_copy(m_v.at[f], gmean.at[f], st.at[F + f]))
        stores[-1].start()

    swapped(LAST)
    for dc in range(C):
        ref = ox.at[LAST, dc - 1] if dc else od.at[LAST - D1, 0]

        def finish(n, dc=dc, ref=ref):
            value = x_v[back(dc), rows_at(n), :].astype(F32) + ref[rows_at(n), :].astype(F32)
            ref[rows_at(n), :] = value.astype(BF16)

        loop(0, nb, finish, 8)
        save(out, ref, back(dc), st.at[2 * F + C + dc])
    for f in (3, 2, 1, 0):
        mean(f)
    for f in range(F):
        pltpu.make_async_copy(e_v.at[f], nerr.at[0, f], st.at[f]).wait()
    for cp in stores:
        cp.wait()

    def handed(d):
        for f in range(F):
            w_copy(f, d).wait_send()
            q_copy(f, d).wait_send()
            c_copy(f, d).wait_send()
            p_copy(f, d, from_z(d)).wait_send()

    loop(1, half_group, handed)
    for f in range(F):
        p_copy(f, 0, dev).wait_send()
        q_copy(f, 0).wait_send()
    for f in range(1, F):
        for dy in range(1, Y):
            y_copy(f, dy).wait_send()
        for dc in range(1, C):
            loop(0, G, lambda n: k_copy(f, dc, n, dev).wait_send())
    for k in range(8):
        for dc in range(1, C):
            o_copy(k, dc).wait_send()
    for k in (COT, ONE):
        for dy in range(Y):
            for dc in range(C):
                if dy or dc:
                    for q in range(Q):
                        x_copy(k, dy, dc, q).wait_send()


def step(G, M, inp, cot, fac, expo, err):
    F, nb, S = fac.shape
    R, T = inp.shape
    C = T // LANES
    Y = M // C
    NBT = M * nb
    U = B // NBT
    SB = C * nb
    tiled = (S // B) % 16 == 0
    hbm = pl.BlockSpec(memory_space=pl.ANY)
    dma = pltpu.SemaphoreType.DMA
    return pl.pallas_call(
        functools.partial(kernel, G, M),
        out_shape=(
            jax.ShapeDtypeStruct((R, T), BF16),
            jax.ShapeDtypeStruct((R, T), BF16),
            jax.ShapeDtypeStruct(fac.shape, F32),
            jax.ShapeDtypeStruct(err.shape, BF16),
        ),
        in_specs=[hbm, hbm, hbm, pl.BlockSpec(memory_space=pltpu.SMEM), hbm],
        out_specs=(hbm,) * 4,
        scratch_shapes=[
            pltpu.VMEM((C, R, LANES), BF16),
            pltpu.VMEM((C, R, LANES), BF16),
            pltpu.VMEM((F, nb, B * B), BF16),
            pltpu.VMEM((max(NBT * (U * nb + PAD), B * (nb + PAD)), LANES), F32),
            pltpu.VMEM((2, C, NBT * U, nb, LANES), BF16),
            pltpu.VMEM((2, NBT * U, NBT, LANES), BF16),
            pltpu.VMEM((NBT * (B + PAD), LANES), F32),
            pltpu.VMEM((NBT * (B + PAD), LANES), F32),
            pltpu.VMEM((NBT * (B + PAD), LANES), F32),
            pltpu.VMEM((NBT * (B + PAD) if tiled else B, LANES), F32),
            pltpu.VMEM((NBT * (U * SB + PAD), LANES), F32),
            pltpu.VMEM((4, SB * B, LANES), BF16),
            pltpu.VMEM((8, C - 1, R, LANES), BF16),
            pltpu.VMEM((2, C, R, LANES), BF16),
            pltpu.VMEM((F, nb, S), BF16),
            pltpu.VMEM((1, nb, S) if tiled else (G, nb, S), BF16),
            pltpu.VMEM((1, 1, 1, 1, nb, S) if tiled else (F - 1, G, C, Y, nb, S), BF16),
            pltpu.VMEM((nb, B, B), BF16),
            pltpu.VMEM((nb, B, B), BF16),
            pltpu.VMEM((F - 1, Y, C, nb, B, B), BF16),
            pltpu.VMEM((F - 1, Y, C, nb, B, B), BF16),
            pltpu.VMEM((F, G, nb, S), BF16),
            pltpu.VMEM((F, G, nb, S), BF16),
            pltpu.VMEM((F, nb, S), F32),
            dma((2 * C + 1 + F,)),
            dma((2 * F + 2 * C,)),
            dma((2, M, Q)),
            dma((2, M, Q)),
            dma((F, Y)),
            dma((F, Y)),
            dma((F, G // 2)),
            dma((F, G // 2)),
            dma((F, G // 2)),
            dma((F, G // 2)),
            dma((F, C, G)),
            dma((F, C, G)),
            dma((8, C)),
            dma((8, C)),
            dma((F, G // 2)),
            dma((F, G // 2)),
            dma((F, G // 2)),
            dma((F, G // 2)),
        ],
        compiler_params=pltpu.CompilerParams(
            collective_id=0, has_side_effects=True, vmem_limit_bytes=62 * 1024 * 1024
        ),
    )(inp, cot, fac, expo, err)


def solution(mesh):
    G, M = mesh.shape["dev"], mesh.shape["ma"]
    in_specs = (
        P("ma", "dev"),
        P("ma", "dev"),
        P(None, "ma", "dev"),
        P(None, "ma"),
        P("dev", None, "ma", None),
    )
    out_specs = (P("ma", "dev"), P("ma", "dev"), P(None, "ma", "dev"), P("dev", None, "ma", None))
    return jax.shard_map(
        functools.partial(step, G, M), mesh=mesh, in_specs=in_specs, out_specs=out_specs, check_vma=False
    )
```

```python
import functools

import jax
import jax.numpy as jnp
from jax import lax
from jax.experimental import pallas as pl
from jax.experimental.pallas import tpu as pltpu
from jax.sharding import PartitionSpec as P

B = 128
LANES = 128
PAD = 8
Q = 4
LIMIT = 127.0
C0 = 0.7978845608028654
C1 = 0.044715
F32 = jnp.float32
BF16 = jnp.bfloat16
MESH = pl.DeviceIdType.MESH
COT, ONE = range(2)
HID, D3, M2, D2, B4, M1, D1, LAST = range(8)


def dot(a, b):
    return lax.dot_general(a, b, (((1,), (0,)), ((), ())), preferred_element_type=F32)


def dot_nt(a, b):
    return lax.dot_general(a, b, (((1,), (1,)), ((), ())), preferred_element_type=F32)


def kernel(
    G, M, inp, cot, fac, expo, err, out, igrad, gmean, nerr,
    x_v, c_v, e_v, gs, tx, rx, sf1, sf2, sb3, slp, sl, op, ox, od, fv, wg0, wg, wn0, wt0, wn, wt, cod, crx, m_v,
    ld, st, xs, xr, ys, yr, ws, wr, ps, pr, ks, kr, os, orr, cs_s, cs_r, qs, qr,
):
    F, nb, S = fac.shape
    C = x_v.shape[0]
    Y = M // C
    NBT = M * nb
    U = B // NBT
    CS = S // B
    SB = C * nb
    PITCH = B + PAD
    SLP = U * SB + PAD
    XP = U * nb + PAD
    GP = nb + PAD
    JR = NBT * U // Q
    tiled = CS % 16 == 0
    ma = lax.axis_index("ma")
    dev = lax.axis_index("dev")
    y, c = ma // C, lax.rem(ma, C)
    s0 = y * SB
    sb2 = sf1 if tiled else sf2
    half_group = G // 2
    partner = dev + 1 - 2 * lax.rem(dev, 2)
    line = half_group == 4
    z, x = dev // 2, lax.rem(dev, 2)
    low = z // 2
    pair_z = z + 1 - 2 * lax.rem(z, 2)
    inner = jnp.logical_or(z == 1, z == 2)

    def lanes(h):
        return slice(h * LANES, (h + 1) * LANES)

    def half(dc):
        return lax.rem(c + dc, C)

    def back(dc):
        return lax.rem(c + C - dc, C)

    def at(dy, dc):
        return {"ma": lax.rem(y + dy, Y) * C + lax.rem(c + dc, C)}

    def loop(lo, hi, fn, unroll=1):
        def one(i, _):
            fn(i)
            return 0

        lax.fori_loop(lo, hi, one, 0, unroll=unroll)

    def steps(lo, hi, fn):
        if line:
            for d in range(lo, hi):
                fn(d)
        else:
            loop(lo, hi, fn)

    loads = []
    for h in range(C):
        loads.append(pltpu.make_async_copy(cot.at[:, lanes(h)], c_v.at[h], ld.at[h]))
    for h in range(C):
        loads.append(pltpu.make_async_copy(inp.at[:, lanes(h)], x_v.at[h], ld.at[C + h]))
    loads.append(pltpu.make_async_copy(err.at[0], e_v, ld.at[2 * C]))
    if tiled:
        own = [pltpu.make_async_copy(fac, fv, ld.at[2 * C + 1])]
    else:
        own = [pltpu.make_async_copy(fac.at[0], wg0.at[dev], ld.at[2 * C + 1])]
        for f in range(1, F):
            own.append(pltpu.make_async_copy(fac.at[f], wg.at[f - 1, dev, c, y], ld.at[2 * C + 1 + f]))
    for cp in own:
        cp.start()
    for cp in loads:
        cp.start()

    barrier = pltpu.get_barrier_semaphore()
    for d in range(1, M):
        pl.semaphore_signal(barrier, inc=1, device_id={"ma": lax.rem(ma + d, M)}, device_id_type=MESH)

    def greet(d):
        pl.semaphore_signal(barrier, inc=1, device_id={"dev": lax.rem(dev + d, G)}, device_id_type=MESH)

    loop(1, G, greet)

    def remote(src, dst, send, recv, to):
        return pltpu.make_async_remote_copy(
            src_ref=src, dst_ref=dst, send_sem=send, recv_sem=recv, device_id=to, device_id_type=MESH
        )

    def slot_of(f, g):
        if tiled:
            rows = pl.ds(pl.multiple_of(g * CS, CS), CS)
            return wn0.at[:, rows, :] if f == 0 else wn.at[f - 1, :, c, :, rows, :]
        return wg0.at[g] if f == 0 else wg.at[f - 1, g, c]

    def mine(f):
        if tiled:
            return wn.at[f - 1, y, c, :, pl.ds(pl.multiple_of(dev * CS, CS), CS), :]
        return wg.at[f - 1, dev, c, y]

    def y_copy(f, dy):
        return remote(mine(f), mine(f), ys.at[f, dy], yr.at[f, dy], at(dy, 0))

    def w_copy(f, d):
        return remote(slot_of(f, dev), slot_of(f, dev), ws.at[f, d], wr.at[f, d], {"dev": lax.rem(dev + 2 * d, G)})

    def hop(f, slot, to_z, sent, d):
        return remote(slot_of(f, slot), slot_of(f, slot), ws.at[f, sent], wr.at[f, d], {"dev": to_z * 2 + x})

    def hops(f):
        return [
            functools.partial(hop, f, from_z(1), 3 - z, 3, 3),
            functools.partial(hop, f, from_z(2), pair_z, 4, 2),
            functools.partial(hop, f, from_z(3), pair_z, 5, 3),
        ]

    def p_copy(f, d, slot):
        return remote(slot_of(f, slot), slot_of(f, slot), ps.at[f, d], pr.at[f, d], {"dev": partner})

    def k_copy(f, dc, n, slot):
        return remote(slot_of(f, slot), slot_of(f, slot), ks.at[f, dc, n], kr.at[f, dc, n], at(0, dc))

    def place(d):
        if d == 0:
            return z
        if d == 1:
            return pair_z
        return (2 - low) if d == 2 else (3 - 3 * low)

    def from_z(d):
        return place(d) * 2 + x if line else lax.rem(dev + G - 2 * d, G)

    def from_x(d):
        return place(d) * 2 + 1 - x if line else lax.rem(partner + G - 2 * d, G)

    def spread_on(f, n, slot):
        if f:
            for dc in range(1, C):
                k_copy(f, dc, n, slot).start()

    def forward(f, lo=1, hi=None):
        def one(d):
            w_copy(f, d).wait_recv()
            if line:
                @pl.when(inner)
                def _():
                    hops(f)[d - 1]().start()
            p_copy(f, d, from_z(d)).start()
            spread_on(f, d, from_z(d))

        steps(lo, half_group if hi is None else hi, one)

    def gather(f):
        def one(d):
            p_copy(f, d, from_x(d)).wait_recv()
            spread_on(f, half_group + d, from_x(d))

        steps(0, half_group, one)

    def push(f):
        if f:
            for dy in range(1, Y):
                y_copy(f, dy).wait_recv()
        if line:
            hop(f, dev, pair_z, 1, 1).start()

            @pl.when(inner)
            def _():
                hop(f, dev, 3 - z, 2, 2).start()
        else:
            loop(1, half_group, lambda d: w_copy(f, d).start())

    def pair(f):
        p_copy(f, 0, dev).start()
        spread_on(f, 0, dev)

    def x_copy(k, dy, dc, q):
        jq = lax.rem(lax.rem(y + dy, Y) * (Q // Y) + q, Q)
        rows = pl.ds(pl.multiple_of(jq * JR, JR), JR)
        return remote(
            tx.at[k, dc, rows], rx.at[k, rows, pl.ds(pl.multiple_of(ma * nb, nb), nb), :],
            xs.at[k, dy * C + dc, q], xr.at[k, dy * C + dc, q], at(dy, dc),
        )

    def chunk(q):
        return lax.rem(y * (Q // Y) + q, Q)

    def arrive(k, q):
        for dy in range(Y):
            for dc in range(C):
                if dy or dc:
                    x_copy(k, dy, dc, q).wait_recv()

    def launch(k, dc, qs_):
        for q in qs_:
            for dy in range(1, Y):
                x_copy(k, dy, dc, q).start()

    def near(k, dc):
        if dc:
            for q in range(Q):
                x_copy(k, 0, dc, q).start()

    def o_copy(k, dc):
        blocks = half(dc) * nb
        if k < B4:
            src = op.at[k, pl.ds(pl.multiple_of(blocks * B, B), nb * B), :]
        elif k < D1:
            src = rx.at[COT if k == B4 else ONE, pl.ds(pl.multiple_of((s0 + blocks) * U, U), nb * U)]
        else:
            src = od.at[k - D1, dc]
        dst = ox.at[k, dc - 1]
        if B4 <= k < D1:
            dst = dst.reshape(nb * U, NBT, LANES)
        return remote(src, dst, os.at[k, dc], orr.at[k, dc], at(0, dc))

    def swap(k):
        for dc in range(1, C):
            o_copy(k, dc).start()

    def swapped(k):
        for dc in range(1, C):
            o_copy(k, dc).wait_recv()

    def q_copy(f, d):
        return remote(cod.at[f, d], crx.at[f, half_group + d], qs.at[f, d], qr.at[f, d], {"dev": partner})

    def c_copy(f, d):
        return remote(
            cod.at[f, half_group + d], crx.at[f, d], cs_s.at[f, d], cs_r.at[f, d], {"dev": lax.rem(dev + 2 * d, G)}
        )

    def combine(f):
        def one(d):
            q_copy(f, d).wait_recv()
            both = cod[f, half_group + d].astype(F32) + crx[f, half_group + d].astype(F32)
            cod[f, half_group + d] = both.astype(BF16)
            c_copy(f, d).start()

        loop(1, half_group, one)
        q_copy(f, 0).wait_recv()
        crx[f, 0] = (cod[f, half_group].astype(F32) + crx[f, half_group].astype(F32)).astype(BF16)

    def scatter(i, value):
        for u in range(U):
            gs[pl.ds(u * nb + i, NBT, stride=XP), :] = value[u * NBT:(u + 1) * NBT]

    def pack(k, dc):
        def one(j):
            rows = gs[pl.ds(pl.multiple_of(j * XP, 8), U * nb), :]
            value = rows.astype(BF16).reshape(U, nb, LANES)
            to = pl.ds(pl.multiple_of(j * U, U), U)
            tx[k, dc, to] = value
            if dc == 0:
                rx[k, to, pl.ds(pl.multiple_of(ma * nb, nb), nb), :] = value

        loop(0, NBT, one, 8)

    def rows_at(n):
        return pl.ds(pl.multiple_of(n * B, B), B)

    def block(k, j):
        return rx[k, pl.ds(j * U, U)].reshape(B, LANES)

    def gathered(ref, i, pitch, step):
        return jnp.concatenate([ref[pl.ds(u * step + i, NBT, stride=pitch), :] for u in range(U)], axis=0)

    def stored(ref, j, value):
        ref[pl.ds(pl.multiple_of(j * PITCH, 8), B), :] = value

    def take_side(k, ref):
        def one(p):
            op[k, rows_at(p), :] = gathered(ref, s0 + p, PITCH, NBT).astype(BF16)

        loop(0, SB, one, 8)

    def taken(k, ref, p, i, side):
        return op[k, rows_at(p), :] if side else gathered(ref, i, PITCH, NBT).astype(BF16)

    def widen(piece):
        def one(g):
            for s in range(CS):
                to = pl.multiple_of((g * CS + s) * GP, 8)
                gs[pl.ds(to, nb), :] = piece(g, s)

        loop(0, G, one)

    def arrange():
        for cp in own:
            cp.wait()
        if tiled:
            for f in range(F):
                for s in range(CS):
                    gs[(f * CS + s) * GP:(f * CS + s) * GP + nb, :] = fv[f, :, s * B:(s + 1) * B].astype(F32)
            for f in range(F):
                def one(n, f=f):
                    tile = gs[pl.ds(f * CS * GP + n, CS, stride=GP), :].astype(BF16)
                    rows = pl.ds(pl.multiple_of(dev * CS, CS), CS)
                    if f:
                        wn[f - 1, y, c, n, rows, :] = tile
                    else:
                        wn0[n, rows, :] = tile

                loop(0, nb, one, 4)

    def weights_first():
        if not tiled:
            widen(lambda g, s: wg0[g, :, s * B:(s + 1) * B].astype(F32))

        def take(n):
            if not tiled:
                wn0[n] = gs[pl.ds(n, B, stride=GP), :].astype(BF16)
            wt0[n] = wn0[n].T

        loop(0, nb, take, 8)

    def landed(f):
        for dc in range(1, C):
            def came(n, dc=dc):
                k_copy(f, dc, n, dev).wait_recv()

            loop(0, G, came)

    def flip(f):
        def group(m):
            yy, cc = m // C, lax.rem(m, C)
            if not tiled:
                widen(lambda g, s: wg[f - 1, g, cc, yy, :, s * B:(s + 1) * B].astype(F32))

            def take(n):
                if not tiled:
                    wn[f - 1, yy, cc, n] = gs[pl.ds(n, B, stride=GP), :].astype(BF16)
                wt[f - 1, yy, cc, n] = wn[f - 1, yy, cc, n].T

            loop(0, nb, take, 8)

        loop(0, M, group)

    def weights(f):
        landed(f)
        flip(f)

    def weight(ref, f, j):
        return ref[f - 1, j // SB, lax.rem(j, SB) // nb, lax.rem(j, nb)]

    def side_weight(ref, f, j):
        at_j = ref.at[f - 1, j // SB, lax.rem(j, SB) // nb, lax.rem(j, nb)]
        rows = [at_j[pl.ds(pl.multiple_of(u * NBT + s0, nb), SB), :] for u in range(U)]
        return jnp.concatenate(rows, axis=0)

    def gradient(f, left, right):
        def one(n):
            a = jnp.concatenate([left(dc, n) for dc in range(C)], axis=1)
            b = jnp.concatenate([right(dc, n) for dc in range(C)], axis=1)
            gs[pl.ds(n, B, stride=GP), :] = dot_nt(a, b)

        loop(0, nb, one, 8)
        row = lax.broadcasted_iota(jnp.int32, (nb, B), 0)
        power = jnp.zeros((nb, B), jnp.int32)
        for n in range(nb):
            power = jnp.where(row == n, expo[f, n], power)
        scale = jnp.left_shift(jnp.ones_like(power), -power).astype(F32)
        inverse = jnp.left_shift(jnp.ones_like(power), 24 + power).astype(F32) * (2.0 ** -24)

        def quantize(g, slot):
            for s in range(CS):
                col = pl.ds(pl.multiple_of((g * CS + s) * B, B), B)
                total = gs[pl.ds(pl.multiple_of((g * CS + s) * GP, 8), nb), :] + e_v[f, :, col].astype(F32)
                code = jnp.clip(total * scale, -LIMIT, LIMIT)
                e_v[f, :, col] = (total - code * inverse).astype(BF16)
                cod[f, slot, :, s * B:(s + 1) * B] = code.astype(BF16)

        def away(step):
            d = lax.rem(step + 1, half_group)
            quantize(lax.rem(partner + 2 * d, G), d)
            q_copy(f, d).start()

        loop(0, half_group, away)
        loop(0, half_group, lambda d: quantize(lax.rem(dev + 2 * d, G), half_group + d))
        pltpu.make_async_copy(e_v.at[f], nerr.at[0, f], st.at[f]).start()
        return inverse

    def op_rows(k, dc, n):
        if dc:
            return ox[k, dc - 1, rows_at(n), :]
        if k < B4:
            return op[k, rows_at(c * nb + n), :]
        if k < D1:
            return block(COT if k == B4 else ONE, ma * nb + n)
        return od[k - D1, 0, rows_at(n), :]

    def ops(k):
        return functools.partial(op_rows, k)

    def spread_cot(dc):
        loop(0, nb, lambda i: scatter(i, c_v[half(dc), rows_at(i), :].astype(F32)), 8)
        pack(COT, dc)

    early, late = tuple(range(Q // Y)), tuple(range(Q // Y, Q))
    arrange()
    pl.semaphore_wait(barrier, M - 1 + G - 1)
    push(0)
    pair(0)
    for f in range(1, F):
        for dy in range(1, Y):
            y_copy(f, dy).start()
    for h in range(C):
        loads[h].wait()
    for dc in range(C - 1, -1, -1):
        spread_cot(dc)
        launch(COT, dc, early)
        near(COT, dc)

    forward(0)
    push(1)
    pair(1)
    push(2)
    push(3)
    gather(0)
    weights_first()
    for h in range(C):
        loads[C + h].wait()
    for dc in range(C - 1, -1, -1):
        loop(0, nb, lambda i: scatter(i, dot(wt0[i], x_v[half(dc), rows_at(i), :])), 8)
        pack(ONE, dc)
        launch(ONE, dc, range(Q))
        near(ONE, dc)
    for dc in range(C - 1, -1, -1):
        launch(COT, dc, late)
    forward(1, 1, 2)
    pair(2)
    forward(1, 2)
    forward(2, 1, 2)
    gather(1)
    pair(3)
    forward(2, 2)
    weights(1)
    for q in early:
        arrive(COT, q)
    swap(B4)

    def first(q):
        arrive(ONE, q)
        base = chunk(q) * (NBT // Q)
        loop(0, NBT // Q, lambda n: stored(sf1, base + n, dot(weight(wt, 1, base + n), block(ONE, base + n))), 8)

    forward(3, 1, 2)
    gather(2)
    forward(3, 2)
    weights(2)
    for q in early:
        first(q)
    swap(M1)
    for q in late:
        first(q)

    def middle(p, side):
        i = lax.rem(s0 + p, NBT)
        v = gathered(sf1, i, PITCH, NBT).astype(BF16).astype(F32)
        square = v * v
        t = jnp.tanh(C0 * (v + C1 * (square * v)))
        halved = 0.5 * (1.0 + t)
        hidden = (v * halved).astype(BF16)
        slope = halved + 0.5 * v * (1.0 - t * t) * (C0 * (1.0 + 3.0 * C1 * square))
        if tiled:
            stored(slp, i, slope)
        else:
            for u in range(U):
                sf1[pl.ds(u * NBT + i, NBT, stride=PITCH), :] = slope[u * NBT:(u + 1) * NBT]
        if side:
            op[HID, rows_at(p), :] = hidden
        stored(sf2, i, dot(weight(wt, 2, i), hidden))

    loop(0, SB, lambda p: middle(p, True), 8)
    swap(HID)
    loop(SB, NBT, lambda p: middle(p, False), 8)
    take_side(M2, sf2)
    swap(M2)
    loads[2 * C].wait()
    inverses = {}
    swapped(M2)
    swapped(B4)
    inverses[3] = gradient(3, ops(M2), ops(B4))
    gather(3)
    landed(3)

    def collect(k):
        for dc in range(C - 1, -1, -1):
            def one(n, dc=dc):
                value = gathered(sl, half(dc) * nb + n, SLP, SB)
                od[k - D1, dc, rows_at(n), :] = value.astype(BF16)

            loop(0, nb, one, 8)
            if dc:
                o_copy(k, dc).start()

    def fourth(p, side):
        j = lax.rem(s0 + p, NBT)
        two = taken(M2, sf2, p, j, side)
        sl[pl.ds(pl.multiple_of(j * SLP, 8), U * SB), :] = dot(side_weight(wt, 3, j), two)

    def last_forward():
        flip(3)
        loop(0, SB, lambda p: fourth(p, True), 8)
        if tiled:
            combine(1)
        loop(SB, NBT, lambda p: fourth(p, False), 8)
        collect(LAST)

    if not tiled:
        last_forward()

    def third_back(q):
        base = chunk(q) * (NBT // Q)
        loop(0, NBT // Q, lambda n: stored(sb3, base + n, dot(weight(wn, 3, base + n), block(COT, base + n))), 8)

    for q in early:
        third_back(q)
    for q in late:
        arrive(COT, q)
        third_back(q)
    take_side(D3, sb3)
    swap(D3)
    combine(3)

    def second_back(p, side):
        i = lax.rem(s0 + p, NBT)
        slope = slp[pl.ds(pl.multiple_of(i * PITCH, 8), B), :] if tiled else gathered(sf1, i, PITCH, NBT)
        stored(sb2, i, dot(weight(wn, 2, i), taken(D3, sb3, p, i, side)) * slope)

    loop(0, SB, lambda p: second_back(p, True), 8)
    swapped(HID)
    swapped(D3)
    inverses[2] = gradient(2, ops(HID), ops(D3))
    loop(SB, NBT, lambda p: second_back(p, False), 8)
    take_side(D2, sb2)
    swap(D2)

    def first_back(p, side):
        j = lax.rem(s0 + p, NBT)
        sl[pl.ds(pl.multiple_of(j * SLP, 8), U * SB), :] = dot(side_weight(wn, 1, j), taken(D2, sb2, p, j, side))

    loop(0, SB, lambda p: first_back(p, True), 8)
    swapped(M1)
    swapped(D2)
    inverses[1] = gradient(1, ops(M1), ops(D2))
    loop(SB, NBT, lambda p: first_back(p, False), 8)
    collect(D1)
    combine(2)
    swapped(D1)
    inverses[0] = gradient(0, lambda dc, n: x_v[back(dc), rows_at(n), :], ops(D1))
    if tiled:
        last_forward()
    else:
        combine(1)
    stores = []

    def save(ref, value_ref, h, sem):
        to = pl.ds(pl.multiple_of(h * LANES, LANES), LANES)
        stores.append(pltpu.make_async_copy(value_ref, ref.at[:, to], sem))
        stores[-1].start()

    for dc in range(C):
        def last_back(n, dc=dc):
            h = back(dc)
            value = c_v[h, rows_at(n), :].astype(F32) + dot(wn0[n], op_rows(D1, dc, n))
            c_v[h, rows_at(n), :] = value.astype(BF16)

        loop(0, nb, last_back, 8)
        save(igrad, c_v.at[back(dc)], back(dc), st.at[2 * F + dc])
    combine(0)

    def mean(f):
        loop(1, half_group, lambda d: c_copy(f, d).wait_recv())

        def column(s):
            col = pl.ds(pl.multiple_of(s * B, B), B)
            total = crx[f, 0, :, col].astype(F32)
            for g in range(1, half_group):
                total = total + crx[f, g, :, col].astype(F32)
            m_v[f, :, col] = total * inverses[f] / G

        loop(0, CS, column)
        stores.append(pltpu.make_async_copy(m_v.at[f], gmean.at[f], st.at[F + f]))
        stores[-1].start()

    swapped(LAST)
    for dc in range(C):
        ref = ox.at[LAST, dc - 1] if dc else od.at[LAST - D1, 0]

        def finish(n, dc=dc, ref=ref):
            value = x_v[back(dc), rows_at(n), :].astype(F32) + ref[rows_at(n), :].astype(F32)
            ref[rows_at(n), :] = value.astype(BF16)

        loop(0, nb, finish, 8)
        save(out, ref, back(dc), st.at[2 * F + C + dc])
    for f in (3, 2, 1, 0):
        mean(f)
    for f in range(F):
        pltpu.make_async_copy(e_v.at[f], nerr.at[0, f], st.at[f]).wait()
    for cp in stores:
        cp.wait()

    def handed(d):
        for f in range(F):
            if not line:
                w_copy(f, d).wait_send()
            q_copy(f, d).wait_send()
            c_copy(f, d).wait_send()
            p_copy(f, d, from_z(d)).wait_send()

    steps(1, half_group, handed)
    if line:
        for f in range(F):
            hop(f, dev, pair_z, 1, 1).wait_send()

        @pl.when(inner)
        def _():
            for f in range(F):
                hop(f, dev, 3 - z, 2, 2).wait_send()
                for copy in hops(f):
                    copy().wait_send()
    for f in range(F):
        p_copy(f, 0, dev).wait_send()
        q_copy(f, 0).wait_send()
    for f in range(1, F):
        for dy in range(1, Y):
            y_copy(f, dy).wait_send()
        for dc in range(1, C):
            loop(0, G, lambda n: k_copy(f, dc, n, dev).wait_send())
    for k in range(8):
        for dc in range(1, C):
            o_copy(k, dc).wait_send()
    for k in (COT, ONE):
        for dy in range(Y):
            for dc in range(C):
                if dy or dc:
                    for q in range(Q):
                        x_copy(k, dy, dc, q).wait_send()


def step(G, M, inp, cot, fac, expo, err):
    F, nb, S = fac.shape
    R, T = inp.shape
    C = T // LANES
    Y = M // C
    NBT = M * nb
    U = B // NBT
    SB = C * nb
    tiled = (S // B) % 16 == 0
    hbm = pl.BlockSpec(memory_space=pl.ANY)
    dma = pltpu.SemaphoreType.DMA
    return pl.pallas_call(
        functools.partial(kernel, G, M),
        out_shape=(
            jax.ShapeDtypeStruct((R, T), BF16),
            jax.ShapeDtypeStruct((R, T), BF16),
            jax.ShapeDtypeStruct(fac.shape, F32),
            jax.ShapeDtypeStruct(err.shape, BF16),
        ),
        in_specs=[hbm, hbm, hbm, pl.BlockSpec(memory_space=pltpu.SMEM), hbm],
        out_specs=(hbm,) * 4,
        scratch_shapes=[
            pltpu.VMEM((C, R, LANES), BF16),
            pltpu.VMEM((C, R, LANES), BF16),
            pltpu.VMEM((F, nb, B * B), BF16),
            pltpu.VMEM((max(NBT * (U * nb + PAD), B * (nb + PAD)), LANES), F32),
            pltpu.VMEM((2, C, NBT * U, nb, LANES), BF16),
            pltpu.VMEM((2, NBT * U, NBT, LANES), BF16),
            pltpu.VMEM((NBT * (B + PAD), LANES), F32),
            pltpu.VMEM((NBT * (B + PAD), LANES), F32),
            pltpu.VMEM((NBT * (B + PAD), LANES), F32),
            pltpu.VMEM((NBT * (B + PAD) if tiled else B, LANES), F32),
            pltpu.VMEM((NBT * (U * SB + PAD), LANES), F32),
            pltpu.VMEM((4, SB * B, LANES), BF16),
            pltpu.VMEM((8, C - 1, R, LANES), BF16),
            pltpu.VMEM((2, C, R, LANES), BF16),
            pltpu.VMEM((F, nb, S), BF16),
            pltpu.VMEM((1, nb, S) if tiled else (G, nb, S), BF16),
            pltpu.VMEM((1, 1, 1, 1, nb, S) if tiled else (F - 1, G, C, Y, nb, S), BF16),
            pltpu.VMEM((nb, B, B), BF16),
            pltpu.VMEM((nb, B, B), BF16),
            pltpu.VMEM((F - 1, Y, C, nb, B, B), BF16),
            pltpu.VMEM((F - 1, Y, C, nb, B, B), BF16),
            pltpu.VMEM((F, G, nb, S), BF16),
            pltpu.VMEM((F, G, nb, S), BF16),
            pltpu.VMEM((F, nb, S), F32),
            dma((2 * C + 1 + F,)),
            dma((2 * F + 2 * C,)),
            dma((2, M, Q)),
            dma((2, M, Q)),
            dma((F, Y)),
            dma((F, Y)),
            dma((F, max(G // 2, 6))),
            dma((F, G // 2)),
            dma((F, G // 2)),
            dma((F, G // 2)),
            dma((F, C, G)),
            dma((F, C, G)),
            dma((8, C)),
            dma((8, C)),
            dma((F, G // 2)),
            dma((F, G // 2)),
            dma((F, G // 2)),
            dma((F, G // 2)),
        ],
        compiler_params=pltpu.CompilerParams(
            collective_id=0, has_side_effects=True, vmem_limit_bytes=62 * 1024 * 1024
        ),
    )(inp, cot, fac, expo, err)


def solution(mesh):
    G, M = mesh.shape["dev"], mesh.shape["ma"]
    in_specs = (
        P("ma", "dev"),
        P("ma", "dev"),
        P(None, "ma", "dev"),
        P(None, "ma"),
        P("dev", None, "ma", None),
    )
    out_specs = (P("ma", "dev"), P("ma", "dev"), P(None, "ma", "dev"), P("dev", None, "ma", None))
    return jax.shard_map(
        functools.partial(step, G, M), mesh=mesh, in_specs=in_specs, out_specs=out_specs, check_vma=False
    )
```

```python
import functools

import jax
import jax.numpy as jnp
from jax import lax
from jax.experimental import pallas as pl
from jax.experimental.pallas import tpu as pltpu
from jax.sharding import PartitionSpec as P

B = 128
LANES = 128
PAD = 8
Q = 4
LIMIT = 127.0
C0 = 0.7978845608028654
C1 = 0.044715
F32 = jnp.float32
BF16 = jnp.bfloat16
MESH = pl.DeviceIdType.MESH
COT, ONE = range(2)
HID, D3, M2, D2, B4, M1, D1, LAST = range(8)


def dot(a, b):
    return lax.dot_general(a, b, (((1,), (0,)), ((), ())), preferred_element_type=F32)


def dot_nt(a, b):
    return lax.dot_general(a, b, (((1,), (1,)), ((), ())), preferred_element_type=F32)


def kernel(
    G, M, inp, cot, fac, expo, err, out, igrad, gmean, nerr,
    x_v, c_v, e_v, gs, tx, rx, sf1, sf2, sb3, slp, sl, op, ox, od, fv, wg0, wg, wn0, wt0, wn, wt, cod, crx, m_v,
    ld, st, xs, xr, ys, yr, ws, wr, ps, pr, ks, kr, os, orr, cs_s, cs_r, qs, qr,
):
    F, nb, S = fac.shape
    C = x_v.shape[0]
    Y = M // C
    NBT = M * nb
    U = B // NBT
    CS = S // B
    SB = C * nb
    PITCH = B + PAD
    SLP = U * SB + PAD
    XP = U * nb + PAD
    GP = nb + PAD
    JR = NBT * U // Q
    tiled = CS % 16 == 0
    ma = lax.axis_index("ma")
    dev = lax.axis_index("dev")
    y, c = ma // C, lax.rem(ma, C)
    s0 = y * SB
    sb2 = sf1 if tiled else sf2
    half_group = G // 2
    partner = dev + 1 - 2 * lax.rem(dev, 2)
    line = half_group == 4
    z, x = dev // 2, lax.rem(dev, 2)
    low = z // 2
    pair_z = z + 1 - 2 * lax.rem(z, 2)
    inner = jnp.logical_or(z == 1, z == 2)

    def lanes(h):
        return slice(h * LANES, (h + 1) * LANES)

    def half(dc):
        return lax.rem(c + dc, C)

    def back(dc):
        return lax.rem(c + C - dc, C)

    def at(dy, dc):
        return {"ma": lax.rem(y + dy, Y) * C + lax.rem(c + dc, C)}

    def loop(lo, hi, fn, unroll=1):
        def one(i, _):
            fn(i)
            return 0

        lax.fori_loop(lo, hi, one, 0, unroll=unroll)

    def steps(lo, hi, fn):
        if line:
            for d in range(lo, hi):
                fn(d)
        else:
            loop(lo, hi, fn)

    loads = []
    for h in range(C):
        loads.append(pltpu.make_async_copy(cot.at[:, lanes(h)], c_v.at[h], ld.at[h]))
    for h in range(C):
        loads.append(pltpu.make_async_copy(inp.at[:, lanes(h)], x_v.at[h], ld.at[C + h]))
    loads.append(pltpu.make_async_copy(err.at[0], e_v, ld.at[2 * C]))
    if tiled:
        own = [pltpu.make_async_copy(fac, fv, ld.at[2 * C + 1])]
    else:
        own = [pltpu.make_async_copy(fac.at[0], wg0.at[dev], ld.at[2 * C + 1])]
        for f in range(1, F):
            own.append(pltpu.make_async_copy(fac.at[f], wg.at[f - 1, dev, c, y], ld.at[2 * C + 1 + f]))
    for cp in own:
        cp.start()
    for cp in loads:
        cp.start()

    barrier = pltpu.get_barrier_semaphore()
    for d in range(1, M):
        pl.semaphore_signal(barrier, inc=1, device_id={"ma": lax.rem(ma + d, M)}, device_id_type=MESH)

    def greet(d):
        pl.semaphore_signal(barrier, inc=1, device_id={"dev": lax.rem(dev + d, G)}, device_id_type=MESH)

    loop(1, G, greet)

    def remote(src, dst, send, recv, to):
        return pltpu.make_async_remote_copy(
            src_ref=src, dst_ref=dst, send_sem=send, recv_sem=recv, device_id=to, device_id_type=MESH
        )

    def slot_of(f, g):
        if tiled:
            rows = pl.ds(pl.multiple_of(g * CS, CS), CS)
            return wn0.at[:, rows, :] if f == 0 else wn.at[f - 1, :, c, :, rows, :]
        return wg0.at[g] if f == 0 else wg.at[f - 1, g, c]

    def mine(f):
        if tiled:
            return wn.at[f - 1, y, c, :, pl.ds(pl.multiple_of(dev * CS, CS), CS), :]
        return wg.at[f - 1, dev, c, y]

    def y_copy(f, dy):
        return remote(mine(f), mine(f), ys.at[f, dy], yr.at[f, dy], at(dy, 0))

    def w_copy(f, d):
        return remote(slot_of(f, dev), slot_of(f, dev), ws.at[f, d], wr.at[f, d], {"dev": lax.rem(dev + 2 * d, G)})

    def hop(f, slot, to_z, sent, d):
        return remote(slot_of(f, slot), slot_of(f, slot), ws.at[f, sent], wr.at[f, d], {"dev": to_z * 2 + x})

    def hops(f):
        return [
            functools.partial(hop, f, from_z(1), 3 - z, 3, 3),
            functools.partial(hop, f, from_z(2), pair_z, 4, 2),
            functools.partial(hop, f, from_z(3), pair_z, 5, 3),
        ]

    def p_copy(f, d, slot):
        return remote(slot_of(f, slot), slot_of(f, slot), ps.at[f, d], pr.at[f, d], {"dev": partner})

    def k_copy(f, dc, n, slot):
        return remote(slot_of(f, slot), slot_of(f, slot), ks.at[f, dc, n], kr.at[f, dc, n], at(0, dc))

    def place(d):
        if d == 0:
            return z
        if d == 1:
            return pair_z
        return (2 - low) if d == 2 else (3 - 3 * low)

    def from_z(d):
        return place(d) * 2 + x if line else lax.rem(dev + G - 2 * d, G)

    def from_x(d):
        return place(d) * 2 + 1 - x if line else lax.rem(partner + G - 2 * d, G)

    def spread_on(f, n, slot):
        if f:
            for dc in range(1, C):
                k_copy(f, dc, n, slot).start()

    def forward(f, lo=1, hi=None):
        def one(d):
            w_copy(f, d).wait_recv()
            if line:
                @pl.when(inner)
                def _():
                    hops(f)[d - 1]().start()
            p_copy(f, d, from_z(d)).start()
            spread_on(f, d, from_z(d))

        steps(lo, half_group if hi is None else hi, one)

    def gather(f):
        def one(d):
            p_copy(f, d, from_x(d)).wait_recv()
            spread_on(f, half_group + d, from_x(d))

        steps(0, half_group, one)

    def push(f):
        if f:
            for dy in range(1, Y):
                y_copy(f, dy).wait_recv()
        if line:
            hop(f, dev, pair_z, 1, 1).start()

            @pl.when(inner)
            def _():
                hop(f, dev, 3 - z, 2, 2).start()
        else:
            loop(1, half_group, lambda d: w_copy(f, d).start())

    def pair(f):
        p_copy(f, 0, dev).start()
        spread_on(f, 0, dev)

    def x_copy(k, dy, dc, q):
        jq = lax.rem(lax.rem(y + dy, Y) * (Q // Y) + q, Q)
        rows = pl.ds(pl.multiple_of(jq * JR, JR), JR)
        return remote(
            tx.at[k, dc, rows], rx.at[k, rows, pl.ds(pl.multiple_of(ma * nb, nb), nb), :],
            xs.at[k, dy * C + dc, q], xr.at[k, dy * C + dc, q], at(dy, dc),
        )

    def chunk(q):
        return lax.rem(y * (Q // Y) + q, Q)

    def arrive(k, q):
        for dy in range(Y):
            for dc in range(C):
                if dy or dc:
                    x_copy(k, dy, dc, q).wait_recv()

    def launch(k, dc, qs_):
        for q in qs_:
            for dy in range(1, Y):
                x_copy(k, dy, dc, q).start()

    def near(k, dc):
        if dc:
            for q in range(Q):
                x_copy(k, 0, dc, q).start()

    def o_copy(k, dc):
        blocks = half(dc) * nb
        if k < B4:
            src = op.at[k, pl.ds(pl.multiple_of(blocks * B, B), nb * B), :]
        elif k < D1:
            src = rx.at[COT if k == B4 else ONE, pl.ds(pl.multiple_of((s0 + blocks) * U, U), nb * U)]
        else:
            src = od.at[k - D1, dc]
        dst = ox.at[k, dc - 1]
        if B4 <= k < D1:
            dst = dst.reshape(nb * U, NBT, LANES)
        return remote(src, dst, os.at[k, dc], orr.at[k, dc], at(0, dc))

    def swap(k):
        for dc in range(1, C):
            o_copy(k, dc).start()

    def swapped(k):
        for dc in range(1, C):
            o_copy(k, dc).wait_recv()

    def q_copy(f, d):
        return remote(cod.at[f, d], crx.at[f, half_group + d], qs.at[f, d], qr.at[f, d], {"dev": partner})

    def c_copy(f, d):
        return remote(
            cod.at[f, half_group + d], crx.at[f, d], cs_s.at[f, d], cs_r.at[f, d], {"dev": lax.rem(dev + 2 * d, G)}
        )

    def combine(f, lo=1, hi=None, ending=True):
        def one(d):
            q_copy(f, d).wait_recv()
            both = cod[f, half_group + d].astype(F32) + crx[f, half_group + d].astype(F32)
            cod[f, half_group + d] = both.astype(BF16)
            c_copy(f, d).start()

        loop(lo, half_group if hi is None else hi, one)
        if ending:
            q_copy(f, 0).wait_recv()
            crx[f, 0] = (cod[f, half_group].astype(F32) + crx[f, half_group].astype(F32)).astype(BF16)

    def scatter(i, value):
        for u in range(U):
            gs[pl.ds(u * nb + i, NBT, stride=XP), :] = value[u * NBT:(u + 1) * NBT]

    def pack(k, dc):
        def one(j):
            rows = gs[pl.ds(pl.multiple_of(j * XP, 8), U * nb), :]
            value = rows.astype(BF16).reshape(U, nb, LANES)
            to = pl.ds(pl.multiple_of(j * U, U), U)
            tx[k, dc, to] = value
            if dc == 0:
                rx[k, to, pl.ds(pl.multiple_of(ma * nb, nb), nb), :] = value

        loop(0, NBT, one, 8)

    def rows_at(n):
        return pl.ds(pl.multiple_of(n * B, B), B)

    def block(k, j):
        return rx[k, pl.ds(j * U, U)].reshape(B, LANES)

    def gathered(ref, i, pitch, step):
        return jnp.concatenate([ref[pl.ds(u * step + i, NBT, stride=pitch), :] for u in range(U)], axis=0)

    def stored(ref, j, value):
        ref[pl.ds(pl.multiple_of(j * PITCH, 8), B), :] = value

    def take_side(k, ref):
        def one(p):
            op[k, rows_at(p), :] = gathered(ref, s0 + p, PITCH, NBT).astype(BF16)

        loop(0, SB, one, 8)

    def taken(k, ref, p, i, side):
        return op[k, rows_at(p), :] if side else gathered(ref, i, PITCH, NBT).astype(BF16)

    def widen(piece):
        def one(g):
            for s in range(CS):
                to = pl.multiple_of((g * CS + s) * GP, 8)
                gs[pl.ds(to, nb), :] = piece(g, s)

        loop(0, G, one)

    def arrange():
        for cp in own:
            cp.wait()
        if tiled:
            for f in range(F):
                for s in range(CS):
                    gs[(f * CS + s) * GP:(f * CS + s) * GP + nb, :] = fv[f, :, s * B:(s + 1) * B].astype(F32)
            for f in range(F):
                def one(n, f=f):
                    tile = gs[pl.ds(f * CS * GP + n, CS, stride=GP), :].astype(BF16)
                    rows = pl.ds(pl.multiple_of(dev * CS, CS), CS)
                    if f:
                        wn[f - 1, y, c, n, rows, :] = tile
                    else:
                        wn0[n, rows, :] = tile

                loop(0, nb, one, 4)

    def weights_first():
        if not tiled:
            widen(lambda g, s: wg0[g, :, s * B:(s + 1) * B].astype(F32))

        def take(n):
            if not tiled:
                wn0[n] = gs[pl.ds(n, B, stride=GP), :].astype(BF16)
            wt0[n] = wn0[n].T

        loop(0, nb, take, 8)

    def landed(f):
        for dc in range(1, C):
            def came(n, dc=dc):
                k_copy(f, dc, n, dev).wait_recv()

            loop(0, G, came)

    def flip(f):
        def group(m):
            yy, cc = m // C, lax.rem(m, C)
            if not tiled:
                widen(lambda g, s: wg[f - 1, g, cc, yy, :, s * B:(s + 1) * B].astype(F32))

            def take(n):
                if not tiled:
                    wn[f - 1, yy, cc, n] = gs[pl.ds(n, B, stride=GP), :].astype(BF16)
                wt[f - 1, yy, cc, n] = wn[f - 1, yy, cc, n].T

            loop(0, nb, take, 8)

        loop(0, M, group)

    def weights(f):
        landed(f)
        flip(f)

    def weight(ref, f, j):
        return ref[f - 1, j // SB, lax.rem(j, SB) // nb, lax.rem(j, nb)]

    def side_weight(ref, f, j):
        at_j = ref.at[f - 1, j // SB, lax.rem(j, SB) // nb, lax.rem(j, nb)]
        rows = [at_j[pl.ds(pl.multiple_of(u * NBT + s0, nb), SB), :] for u in range(U)]
        return jnp.concatenate(rows, axis=0)

    def gradient(f, left, right):
        def one(n):
            a = jnp.concatenate([left(dc, n) for dc in range(C)], axis=1)
            b = jnp.concatenate([right(dc, n) for dc in range(C)], axis=1)
            gs[pl.ds(n, B, stride=GP), :] = dot_nt(a, b)

        loop(0, nb, one, 8)
        row = lax.broadcasted_iota(jnp.int32, (nb, B), 0)
        power = jnp.zeros((nb, B), jnp.int32)
        for n in range(nb):
            power = jnp.where(row == n, expo[f, n], power)
        scale = jnp.left_shift(jnp.ones_like(power), -power).astype(F32)
        inverse = jnp.left_shift(jnp.ones_like(power), 24 + power).astype(F32) * (2.0 ** -24)

        def quantize(g, slot):
            for s in range(CS):
                col = pl.ds(pl.multiple_of((g * CS + s) * B, B), B)
                total = gs[pl.ds(pl.multiple_of((g * CS + s) * GP, 8), nb), :] + e_v[f, :, col].astype(F32)
                code = jnp.clip(total * scale, -LIMIT, LIMIT)
                e_v[f, :, col] = (total - code * inverse).astype(BF16)
                cod[f, slot, :, s * B:(s + 1) * B] = code.astype(BF16)

        def away(step):
            d = lax.rem(step + 1, half_group)
            quantize(lax.rem(partner + 2 * d, G), d)
            q_copy(f, d).start()

        loop(0, half_group, away)
        loop(0, half_group, lambda d: quantize(lax.rem(dev + 2 * d, G), half_group + d))
        pltpu.make_async_copy(e_v.at[f], nerr.at[0, f], st.at[f]).start()
        return inverse

    def op_rows(k, dc, n):
        if dc:
            return ox[k, dc - 1, rows_at(n), :]
        if k < B4:
            return op[k, rows_at(c * nb + n), :]
        if k < D1:
            return block(COT if k == B4 else ONE, ma * nb + n)
        return od[k - D1, 0, rows_at(n), :]

    def ops(k):
        return functools.partial(op_rows, k)

    def spread_cot(dc):
        loop(0, nb, lambda i: scatter(i, c_v[half(dc), rows_at(i), :].astype(F32)), 8)
        pack(COT, dc)

    early, late = tuple(range(Q // Y)), tuple(range(Q // Y, Q))
    arrange()
    pl.semaphore_wait(barrier, M - 1 + G - 1)
    push(0)
    pair(0)
    for f in range(1, F):
        for dy in range(1, Y):
            y_copy(f, dy).start()
    for h in range(C):
        loads[h].wait()
    for dc in range(C - 1, -1, -1):
        spread_cot(dc)
        launch(COT, dc, early)
        near(COT, dc)

    forward(0, 1, 2)
    push(1)
    pair(1)
    forward(0, 2)
    push(2)
    push(3)
    pair(2)
    gather(0)
    weights_first()
    for h in range(C):
        loads[C + h].wait()
    for dc in range(C - 1, -1, -1):
        loop(0, nb, lambda i: scatter(i, dot(wt0[i], x_v[half(dc), rows_at(i), :])), 8)
        pack(ONE, dc)
        launch(ONE, dc, range(Q))
        near(ONE, dc)
    for dc in range(C - 1, -1, -1):
        launch(COT, dc, late)
    forward(1, 1, 2)
    pair(3)
    forward(1, 2)
    forward(2, 1, 2)
    gather(1)
    forward(2, 2)
    weights(1)
    for q in early:
        arrive(COT, q)
    swap(B4)

    def first(q):
        arrive(ONE, q)
        base = chunk(q) * (NBT // Q)
        loop(0, NBT // Q, lambda n: stored(sf1, base + n, dot(weight(wt, 1, base + n), block(ONE, base + n))), 8)

    forward(3, 1, 2)
    gather(2)
    forward(3, 2)
    weights(2)
    for q in early:
        first(q)
    swap(M1)
    for q in late:
        first(q)

    def middle(p, side):
        i = lax.rem(s0 + p, NBT)
        v = gathered(sf1, i, PITCH, NBT).astype(BF16).astype(F32)
        square = v * v
        t = jnp.tanh(C0 * (v + C1 * (square * v)))
        halved = 0.5 * (1.0 + t)
        hidden = (v * halved).astype(BF16)
        slope = halved + 0.5 * v * (1.0 - t * t) * (C0 * (1.0 + 3.0 * C1 * square))
        if tiled:
            stored(slp, i, slope)
        else:
            for u in range(U):
                sf1[pl.ds(u * NBT + i, NBT, stride=PITCH), :] = slope[u * NBT:(u + 1) * NBT]
        if side:
            op[HID, rows_at(p), :] = hidden
        stored(sf2, i, dot(weight(wt, 2, i), hidden))

    loop(0, SB, lambda p: middle(p, True), 8)
    swap(HID)
    loop(SB, NBT, lambda p: middle(p, False), 8)
    take_side(M2, sf2)
    swap(M2)
    loads[2 * C].wait()
    inverses = {}
    swapped(M2)
    swapped(B4)
    inverses[3] = gradient(3, ops(M2), ops(B4))
    gather(3)
    landed(3)

    def collect(k):
        for dc in range(C - 1, -1, -1):
            def one(n, dc=dc):
                value = gathered(sl, half(dc) * nb + n, SLP, SB)
                od[k - D1, dc, rows_at(n), :] = value.astype(BF16)

            loop(0, nb, one, 8)
            if dc:
                o_copy(k, dc).start()

    def fourth(p, side):
        j = lax.rem(s0 + p, NBT)
        two = taken(M2, sf2, p, j, side)
        sl[pl.ds(pl.multiple_of(j * SLP, 8), U * SB), :] = dot(side_weight(wt, 3, j), two)

    def last_forward(polls):
        if tiled:
            polls[0]()
        loop(0, SB, lambda p: fourth(p, True), 8)
        if tiled:
            polls[1]()
        loop(SB, NBT, lambda p: fourth(p, False), 8)
        if tiled:
            polls[2]()
        collect(LAST)

    if not tiled:
        flip(3)
        last_forward(())

    def third_back(q):
        base = chunk(q) * (NBT // Q)
        loop(0, NBT // Q, lambda n: stored(sb3, base + n, dot(weight(wn, 3, base + n), block(COT, base + n))), 8)

    for q in early:
        third_back(q)
    if tiled:
        flip(3)
    for q in late:
        arrive(COT, q)
        third_back(q)
    take_side(D3, sb3)
    swap(D3)
    combine(3)

    def second_back(p, side):
        i = lax.rem(s0 + p, NBT)
        slope = slp[pl.ds(pl.multiple_of(i * PITCH, 8), B), :] if tiled else gathered(sf1, i, PITCH, NBT)
        stored(sb2, i, dot(weight(wn, 2, i), taken(D3, sb3, p, i, side)) * slope)

    loop(0, SB, lambda p: second_back(p, True), 8)
    swapped(HID)
    swapped(D3)
    inverses[2] = gradient(2, ops(HID), ops(D3))
    loop(SB, NBT, lambda p: second_back(p, False), 8)
    take_side(D2, sb2)
    swap(D2)

    def first_back(p, side):
        j = lax.rem(s0 + p, NBT)
        sl[pl.ds(pl.multiple_of(j * SLP, 8), U * SB), :] = dot(side_weight(wn, 1, j), taken(D2, sb2, p, j, side))

    loop(0, SB, lambda p: first_back(p, True), 8)
    swapped(M1)
    swapped(D2)
    inverses[1] = gradient(1, ops(M1), ops(D2))
    loop(SB, NBT, lambda p: first_back(p, False), 8)
    collect(D1)
    combine(2)
    swapped(D1)
    inverses[0] = gradient(0, lambda dc, n: x_v[back(dc), rows_at(n), :], ops(D1))
    if tiled:
        last_forward((
            lambda: combine(1),
            lambda: combine(0, 1, 2, False),
            lambda: combine(0, 2, half_group - 1, False),
        ))
        combine(0, half_group - 1, None, False)
    else:
        combine(1)
    stores = []

    def save(ref, value_ref, h, sem):
        to = pl.ds(pl.multiple_of(h * LANES, LANES), LANES)
        stores.append(pltpu.make_async_copy(value_ref, ref.at[:, to], sem))
        stores[-1].start()

    for dc in range(C):
        def last_back(n, dc=dc):
            h = back(dc)
            value = c_v[h, rows_at(n), :].astype(F32) + dot(wn0[n], op_rows(D1, dc, n))
            c_v[h, rows_at(n), :] = value.astype(BF16)

        loop(0, nb, last_back, 8)
        save(igrad, c_v.at[back(dc)], back(dc), st.at[2 * F + dc])
    if tiled:
        combine(0, half_group)
    else:
        combine(0)

    def mean(f):
        loop(1, half_group, lambda d: c_copy(f, d).wait_recv())

        def column(s):
            col = pl.ds(pl.multiple_of(s * B, B), B)
            total = crx[f, 0, :, col].astype(F32)
            for g in range(1, half_group):
                total = total + crx[f, g, :, col].astype(F32)
            m_v[f, :, col] = total * inverses[f] / G

        loop(0, CS, column)
        stores.append(pltpu.make_async_copy(m_v.at[f], gmean.at[f], st.at[F + f]))
        stores[-1].start()

    swapped(LAST)
    for dc in range(C):
        ref = ox.at[LAST, dc - 1] if dc else od.at[LAST - D1, 0]

        def finish(n, dc=dc, ref=ref):
            value = x_v[back(dc), rows_at(n), :].astype(F32) + ref[rows_at(n), :].astype(F32)
            ref[rows_at(n), :] = value.astype(BF16)

        loop(0, nb, finish, 8)
        save(out, ref, back(dc), st.at[2 * F + C + dc])
    for f in (3, 2, 1, 0):
        mean(f)
    for f in range(F):
        pltpu.make_async_copy(e_v.at[f], nerr.at[0, f], st.at[f]).wait()
    for cp in stores:
        cp.wait()

    def handed(d):
        for f in range(F):
            if not line:
                w_copy(f, d).wait_send()
            q_copy(f, d).wait_send()
            c_copy(f, d).wait_send()
            p_copy(f, d, from_z(d)).wait_send()

    steps(1, half_group, handed)
    if line:
        for f in range(F):
            hop(f, dev, pair_z, 1, 1).wait_send()

        @pl.when(inner)
        def _():
            for f in range(F):
                hop(f, dev, 3 - z, 2, 2).wait_send()
                for copy in hops(f):
                    copy().wait_send()
    for f in range(F):
        p_copy(f, 0, dev).wait_send()
        q_copy(f, 0).wait_send()
    for f in range(1, F):
        for dy in range(1, Y):
            y_copy(f, dy).wait_send()
        for dc in range(1, C):
            loop(0, G, lambda n: k_copy(f, dc, n, dev).wait_send())
    for k in range(8):
        for dc in range(1, C):
            o_copy(k, dc).wait_send()
    for k in (COT, ONE):
        for dy in range(Y):
            for dc in range(C):
                if dy or dc:
                    for q in range(Q):
                        x_copy(k, dy, dc, q).wait_send()


def step(G, M, inp, cot, fac, expo, err):
    F, nb, S = fac.shape
    R, T = inp.shape
    C = T // LANES
    Y = M // C
    NBT = M * nb
    U = B // NBT
    SB = C * nb
    tiled = (S // B) % 16 == 0
    hbm = pl.BlockSpec(memory_space=pl.ANY)
    dma = pltpu.SemaphoreType.DMA
    return pl.pallas_call(
        functools.partial(kernel, G, M),
        out_shape=(
            jax.ShapeDtypeStruct((R, T), BF16),
            jax.ShapeDtypeStruct((R, T), BF16),
            jax.ShapeDtypeStruct(fac.shape, F32),
            jax.ShapeDtypeStruct(err.shape, BF16),
        ),
        in_specs=[hbm, hbm, hbm, pl.BlockSpec(memory_space=pltpu.SMEM), hbm],
        out_specs=(hbm,) * 4,
        scratch_shapes=[
            pltpu.VMEM((C, R, LANES), BF16),
            pltpu.VMEM((C, R, LANES), BF16),
            pltpu.VMEM((F, nb, B * B), BF16),
            pltpu.VMEM((max(NBT * (U * nb + PAD), B * (nb + PAD)), LANES), F32),
            pltpu.VMEM((2, C, NBT * U, nb, LANES), BF16),
            pltpu.VMEM((2, NBT * U, NBT, LANES), BF16),
            pltpu.VMEM((NBT * (B + PAD), LANES), F32),
            pltpu.VMEM((NBT * (B + PAD), LANES), F32),
            pltpu.VMEM((NBT * (B + PAD), LANES), F32),
            pltpu.VMEM((NBT * (B + PAD) if tiled else B, LANES), F32),
            pltpu.VMEM((NBT * (U * SB + PAD), LANES), F32),
            pltpu.VMEM((4, SB * B, LANES), BF16),
            pltpu.VMEM((8, C - 1, R, LANES), BF16),
            pltpu.VMEM((2, C, R, LANES), BF16),
            pltpu.VMEM((F, nb, S), BF16),
            pltpu.VMEM((1, nb, S) if tiled else (G, nb, S), BF16),
            pltpu.VMEM((1, 1, 1, 1, nb, S) if tiled else (F - 1, G, C, Y, nb, S), BF16),
            pltpu.VMEM((nb, B, B), BF16),
            pltpu.VMEM((nb, B, B), BF16),
            pltpu.VMEM((F - 1, Y, C, nb, B, B), BF16),
            pltpu.VMEM((F - 1, Y, C, nb, B, B), BF16),
            pltpu.VMEM((F, G, nb, S), BF16),
            pltpu.VMEM((F, G, nb, S), BF16),
            pltpu.VMEM((F, nb, S), F32),
            dma((2 * C + 1 + F,)),
            dma((2 * F + 2 * C,)),
            dma((2, M, Q)),
            dma((2, M, Q)),
            dma((F, Y)),
            dma((F, Y)),
            dma((F, max(G // 2, 6))),
            dma((F, G // 2)),
            dma((F, G // 2)),
            dma((F, G // 2)),
            dma((F, C, G)),
            dma((F, C, G)),
            dma((8, C)),
            dma((8, C)),
            dma((F, G // 2)),
            dma((F, G // 2)),
            dma((F, G // 2)),
            dma((F, G // 2)),
        ],
        compiler_params=pltpu.CompilerParams(
            collective_id=0, has_side_effects=True, vmem_limit_bytes=62 * 1024 * 1024
        ),
    )(inp, cot, fac, expo, err)


def solution(mesh):
    G, M = mesh.shape["dev"], mesh.shape["ma"]
    in_specs = (
        P("ma", "dev"),
        P("ma", "dev"),
        P(None, "ma", "dev"),
        P(None, "ma"),
        P("dev", None, "ma", None),
    )
    out_specs = (P("ma", "dev"), P("ma", "dev"), P(None, "ma", "dev"), P("dev", None, "ma", None))
    return jax.shard_map(
        functools.partial(step, G, M), mesh=mesh, in_specs=in_specs, out_specs=out_specs, check_vma=False
    )
```

```python
import functools

import jax
import jax.numpy as jnp
from jax import lax
from jax.experimental import pallas as pl
from jax.experimental.pallas import tpu as pltpu
from jax.sharding import PartitionSpec as P

B = 128
LANES = 128
PAD = 8
Q = 4
LIMIT = 127.0
C0 = 0.7978845608028654
C1 = 0.044715
F32 = jnp.float32
BF16 = jnp.bfloat16
MESH = pl.DeviceIdType.MESH
COT, ONE = range(2)
HID, D3, M2, D2, B4, M1, D1, LAST = range(8)


def dot(a, b):
    return lax.dot_general(a, b, (((1,), (0,)), ((), ())), preferred_element_type=F32)


def dot_nt(a, b):
    return lax.dot_general(a, b, (((1,), (1,)), ((), ())), preferred_element_type=F32)


def kernel(
    G, M, inp, cot, fac, expo, err, out, igrad, gmean, nerr,
    x_v, c_v, e_v, gs, tx, rx, sf1, sf2, sb3, slp, sl, op, ox, od, fv, wg0, wg, wn0, wt0, wn, wt, cod, crx, m_v,
    ld, st, xs, xr, ys, yr, ws, wr, ps, pr, ks, kr, os, orr, cs_s, cs_r, qs, qr,
):
    F, nb, S = fac.shape
    C = x_v.shape[0]
    Y = M // C
    NBT = M * nb
    U = B // NBT
    CS = S // B
    SB = C * nb
    PITCH = B + PAD
    SLP = U * SB + PAD
    XP = U * nb + PAD
    GP = nb + PAD
    JR = NBT * U // Q
    tiled = CS % 16 == 0
    ma = lax.axis_index("ma")
    dev = lax.axis_index("dev")
    y, c = ma // C, lax.rem(ma, C)
    s0 = y * SB
    sb2 = sf1 if tiled else sf2
    half_group = G // 2
    partner = dev + 1 - 2 * lax.rem(dev, 2)
    line = half_group == 4
    z, x = dev // 2, lax.rem(dev, 2)
    low = z // 2
    pair_z = z + 1 - 2 * lax.rem(z, 2)
    inner = jnp.logical_or(z == 1, z == 2)

    def lanes(h):
        return slice(h * LANES, (h + 1) * LANES)

    def half(dc):
        return lax.rem(c + dc, C)

    def back(dc):
        return lax.rem(c + C - dc, C)

    def at(dy, dc):
        return {"ma": lax.rem(y + dy, Y) * C + lax.rem(c + dc, C)}

    def loop(lo, hi, fn, unroll=1):
        def one(i, _):
            fn(i)
            return 0

        lax.fori_loop(lo, hi, one, 0, unroll=unroll)

    def steps(lo, hi, fn):
        if line:
            for d in range(lo, hi):
                fn(d)
        else:
            loop(lo, hi, fn)

    loads = []
    for h in range(C):
        loads.append(pltpu.make_async_copy(cot.at[:, lanes(h)], c_v.at[h], ld.at[h]))
    for h in range(C):
        loads.append(pltpu.make_async_copy(inp.at[:, lanes(h)], x_v.at[h], ld.at[C + h]))
    loads.append(pltpu.make_async_copy(err.at[0], e_v, ld.at[2 * C]))
    if tiled:
        own = [pltpu.make_async_copy(fac, fv, ld.at[2 * C + 1])]
    else:
        own = [pltpu.make_async_copy(fac.at[0], wg0.at[dev], ld.at[2 * C + 1])]
        for f in range(1, F):
            own.append(pltpu.make_async_copy(fac.at[f], wg.at[f - 1, dev, c, y], ld.at[2 * C + 1 + f]))
    for cp in own:
        cp.start()
    for cp in loads:
        cp.start()

    barrier = pltpu.get_barrier_semaphore()
    for d in range(1, M):
        pl.semaphore_signal(barrier, inc=1, device_id={"ma": lax.rem(ma + d, M)}, device_id_type=MESH)

    def greet(d):
        pl.semaphore_signal(barrier, inc=1, device_id={"dev": lax.rem(dev + d, G)}, device_id_type=MESH)

    loop(1, G, greet)

    def remote(src, dst, send, recv, to):
        return pltpu.make_async_remote_copy(
            src_ref=src, dst_ref=dst, send_sem=send, recv_sem=recv, device_id=to, device_id_type=MESH
        )

    def slot_of(f, g):
        if tiled:
            rows = pl.ds(pl.multiple_of(g * CS, CS), CS)
            return wn0.at[:, rows, :] if f == 0 else wn.at[f - 1, :, c, :, rows, :]
        return wg0.at[g] if f == 0 else wg.at[f - 1, g, c]

    def mine(f):
        if tiled:
            return wn.at[f - 1, y, c, :, pl.ds(pl.multiple_of(dev * CS, CS), CS), :]
        return wg.at[f - 1, dev, c, y]

    def y_copy(f, dy):
        return remote(mine(f), mine(f), ys.at[f, dy], yr.at[f, dy], at(dy, 0))

    def w_copy(f, d):
        return remote(slot_of(f, dev), slot_of(f, dev), ws.at[f, d], wr.at[f, d], {"dev": lax.rem(dev + 2 * d, G)})

    def hop(f, slot, to_z, sent, d):
        return remote(slot_of(f, slot), slot_of(f, slot), ws.at[f, sent], wr.at[f, d], {"dev": to_z * 2 + x})

    def hops(f):
        return [
            functools.partial(hop, f, from_z(1), 3 - z, 3, 3),
            functools.partial(hop, f, from_z(2), pair_z, 4, 2),
            functools.partial(hop, f, from_z(3), pair_z, 5, 3),
        ]

    def p_copy(f, d, slot):
        return remote(slot_of(f, slot), slot_of(f, slot), ps.at[f, d], pr.at[f, d], {"dev": partner})

    def k_copy(f, dc, n, slot):
        return remote(slot_of(f, slot), slot_of(f, slot), ks.at[f, dc, n], kr.at[f, dc, n], at(0, dc))

    def place(d):
        if d == 0:
            return z
        if d == 1:
            return pair_z
        return (2 - low) if d == 2 else (3 - 3 * low)

    def from_z(d):
        return place(d) * 2 + x if line else lax.rem(dev + G - 2 * d, G)

    def from_x(d):
        return place(d) * 2 + 1 - x if line else lax.rem(partner + G - 2 * d, G)

    def spread_on(f, n, slot):
        if f:
            for dc in range(1, C):
                k_copy(f, dc, n, slot).start()

    def forward(f, lo=1, hi=None):
        def one(d):
            w_copy(f, d).wait_recv()
            if line:
                @pl.when(inner)
                def _():
                    hops(f)[d - 1]().start()
            p_copy(f, d, from_z(d)).start()
            spread_on(f, d, from_z(d))

        steps(lo, half_group if hi is None else hi, one)

    def gather(f):
        def one(d):
            p_copy(f, d, from_x(d)).wait_recv()
            spread_on(f, half_group + d, from_x(d))

        steps(0, half_group, one)

    def push(f):
        if f:
            for dy in range(1, Y):
                y_copy(f, dy).wait_recv()
        if line:
            hop(f, dev, pair_z, 1, 1).start()

            @pl.when(inner)
            def _():
                hop(f, dev, 3 - z, 2, 2).start()
        else:
            loop(1, half_group, lambda d: w_copy(f, d).start())

    def pair(f):
        p_copy(f, 0, dev).start()
        spread_on(f, 0, dev)

    def x_copy(k, dy, dc, q):
        jq = lax.rem(lax.rem(y + dy, Y) * (Q // Y) + q, Q)
        rows = pl.ds(pl.multiple_of(jq * JR, JR), JR)
        return remote(
            tx.at[k, dc, rows], rx.at[k, rows, pl.ds(pl.multiple_of(ma * nb, nb), nb), :],
            xs.at[k, dy * C + dc, q], xr.at[k, dy * C + dc, q], at(dy, dc),
        )

    def chunk(q):
        return lax.rem(y * (Q // Y) + q, Q)

    def arrive(k, q):
        for dy in range(Y):
            for dc in range(C):
                if dy or dc:
                    x_copy(k, dy, dc, q).wait_recv()

    def launch(k, dc, qs_):
        for q in qs_:
            for dy in range(1, Y):
                x_copy(k, dy, dc, q).start()

    def near(k, dc):
        if dc:
            for q in range(Q):
                x_copy(k, 0, dc, q).start()

    def o_copy(k, dc):
        blocks = half(dc) * nb
        if k < B4:
            src = op.at[k, pl.ds(pl.multiple_of(blocks * B, B), nb * B), :]
        elif k < D1:
            src = rx.at[COT if k == B4 else ONE, pl.ds(pl.multiple_of((s0 + blocks) * U, U), nb * U)]
        else:
            src = od.at[k - D1, dc]
        dst = ox.at[k, dc - 1]
        if B4 <= k < D1:
            dst = dst.reshape(nb * U, NBT, LANES)
        return remote(src, dst, os.at[k, dc], orr.at[k, dc], at(0, dc))

    def swap(k):
        for dc in range(1, C):
            o_copy(k, dc).start()

    def swapped(k):
        for dc in range(1, C):
            o_copy(k, dc).wait_recv()

    def q_copy(f, d):
        return remote(cod.at[f, d], crx.at[f, half_group + d], qs.at[f, d], qr.at[f, d], {"dev": partner})

    def c_copy(f, d):
        return remote(
            cod.at[f, half_group + d], crx.at[f, d], cs_s.at[f, d], cs_r.at[f, d], {"dev": lax.rem(dev + 2 * d, G)}
        )

    def combine(f, lo=1, hi=None, ending=True):
        def one(d):
            q_copy(f, d).wait_recv()
            both = cod[f, half_group + d].astype(F32) + crx[f, half_group + d].astype(F32)
            cod[f, half_group + d] = both.astype(BF16)
            c_copy(f, d).start()

        loop(lo, half_group if hi is None else hi, one)
        if ending:
            q_copy(f, 0).wait_recv()
            crx[f, 0] = (cod[f, half_group].astype(F32) + crx[f, half_group].astype(F32)).astype(BF16)

    def scatter(i, value):
        for u in range(U):
            gs[pl.ds(u * nb + i, NBT, stride=XP), :] = value[u * NBT:(u + 1) * NBT]

    def pack(k, dc):
        def one(j):
            rows = gs[pl.ds(pl.multiple_of(j * XP, 8), U * nb), :]
            value = rows.astype(BF16).reshape(U, nb, LANES)
            to = pl.ds(pl.multiple_of(j * U, U), U)
            tx[k, dc, to] = value
            if dc == 0:
                rx[k, to, pl.ds(pl.multiple_of(ma * nb, nb), nb), :] = value

        loop(0, NBT, one, 8)

    def rows_at(n):
        return pl.ds(pl.multiple_of(n * B, B), B)

    def block(k, j):
        return rx[k, pl.ds(j * U, U)].reshape(B, LANES)

    def gathered(ref, i, pitch, step):
        return jnp.concatenate([ref[pl.ds(u * step + i, NBT, stride=pitch), :] for u in range(U)], axis=0)

    def stored(ref, j, value):
        ref[pl.ds(pl.multiple_of(j * PITCH, 8), B), :] = value

    def take_side(k, ref):
        def one(p):
            op[k, rows_at(p), :] = gathered(ref, s0 + p, PITCH, NBT).astype(BF16)

        loop(0, SB, one, 8)

    def taken(k, ref, p, i, side):
        return op[k, rows_at(p), :] if side else gathered(ref, i, PITCH, NBT).astype(BF16)

    def widen(piece):
        def one(g):
            for s in range(CS):
                to = pl.multiple_of((g * CS + s) * GP, 8)
                gs[pl.ds(to, nb), :] = piece(g, s)

        loop(0, G, one)

    def arrange():
        for cp in own:
            cp.wait()
        if tiled:
            for f in range(F):
                for s in range(CS):
                    gs[(f * CS + s) * GP:(f * CS + s) * GP + nb, :] = fv[f, :, s * B:(s + 1) * B].astype(F32)
            for f in range(F):
                def one(n, f=f):
                    tile = gs[pl.ds(f * CS * GP + n, CS, stride=GP), :].astype(BF16)
                    rows = pl.ds(pl.multiple_of(dev * CS, CS), CS)
                    if f:
                        wn[f - 1, y, c, n, rows, :] = tile
                    else:
                        wn0[n, rows, :] = tile

                loop(0, nb, one, 4)

    def weights_first():
        if not tiled:
            widen(lambda g, s: wg0[g, :, s * B:(s + 1) * B].astype(F32))

        def take(n):
            if not tiled:
                wn0[n] = gs[pl.ds(n, B, stride=GP), :].astype(BF16)
            wt0[n] = wn0[n].T

        loop(0, nb, take, 8)

    def landed(f):
        for dc in range(1, C):
            def came(n, dc=dc):
                k_copy(f, dc, n, dev).wait_recv()

            loop(0, G, came)

    def flip(f):
        def group(m):
            yy, cc = m // C, lax.rem(m, C)
            if not tiled:
                widen(lambda g, s: wg[f - 1, g, cc, yy, :, s * B:(s + 1) * B].astype(F32))

            def take(n):
                if not tiled:
                    wn[f - 1, yy, cc, n] = gs[pl.ds(n, B, stride=GP), :].astype(BF16)
                wt[f - 1, yy, cc, n] = wn[f - 1, yy, cc, n].T

            loop(0, nb, take, 8)

        loop(0, M, group)

    def weights(f):
        landed(f)
        flip(f)

    def weight(ref, f, j):
        return ref[f - 1, j // SB, lax.rem(j, SB) // nb, lax.rem(j, nb)]

    def side_weight(ref, f, j):
        at_j = ref.at[f - 1, j // SB, lax.rem(j, SB) // nb, lax.rem(j, nb)]
        rows = [at_j[pl.ds(pl.multiple_of(u * NBT + s0, nb), SB), :] for u in range(U)]
        return jnp.concatenate(rows, axis=0)

    def gradient(f, left, right):
        def one(n):
            a = jnp.concatenate([left(dc, n) for dc in range(C)], axis=1)
            b = jnp.concatenate([right(dc, n) for dc in range(C)], axis=1)
            gs[pl.ds(n, B, stride=GP), :] = dot_nt(a, b)

        loop(0, nb, one, 8)
        row = lax.broadcasted_iota(jnp.int32, (nb, B), 0)
        power = jnp.zeros((nb, B), jnp.int32)
        for n in range(nb):
            power = jnp.where(row == n, expo[f, n], power)
        scale = jnp.left_shift(jnp.ones_like(power), -power).astype(F32)
        inverse = jnp.left_shift(jnp.ones_like(power), 24 + power).astype(F32) * (2.0 ** -24)

        def quantize(g, slot):
            for s in range(CS):
                col = pl.ds(pl.multiple_of((g * CS + s) * B, B), B)
                total = gs[pl.ds(pl.multiple_of((g * CS + s) * GP, 8), nb), :] + e_v[f, :, col].astype(F32)
                code = jnp.clip(total * scale, -LIMIT, LIMIT)
                e_v[f, :, col] = (total - code * inverse).astype(BF16)
                cod[f, slot, :, s * B:(s + 1) * B] = code.astype(BF16)

        def away(step):
            d = lax.rem(step + 1, half_group)
            quantize(lax.rem(partner + 2 * d, G), d)
            q_copy(f, d).start()

        loop(0, half_group, away)
        loop(0, half_group, lambda d: quantize(lax.rem(dev + 2 * d, G), half_group + d))
        pltpu.make_async_copy(e_v.at[f], nerr.at[0, f], st.at[f]).start()
        return inverse

    def op_rows(k, dc, n):
        if dc:
            return ox[k, dc - 1, rows_at(n), :]
        if k < B4:
            return op[k, rows_at(c * nb + n), :]
        if k < D1:
            return block(COT if k == B4 else ONE, ma * nb + n)
        return od[k - D1, 0, rows_at(n), :]

    def ops(k):
        return functools.partial(op_rows, k)

    def spread_cot(dc):
        loop(0, nb, lambda i: scatter(i, c_v[half(dc), rows_at(i), :].astype(F32)), 8)
        pack(COT, dc)

    early, late = tuple(range(Q // Y)), tuple(range(Q // Y, Q))
    arrange()
    pl.semaphore_wait(barrier, M - 1 + G - 1)
    push(0)
    pair(0)
    for f in range(1, F):
        for dy in range(1, Y):
            y_copy(f, dy).start()
    for h in range(C):
        loads[h].wait()
    for dc in range(C - 1, -1, -1):
        spread_cot(dc)
        launch(COT, dc, early)
        near(COT, dc)

    forward(0, 1, 2)
    push(1)
    pair(1)
    forward(0, 2)
    push(2)
    push(3)
    pair(2)
    gather(0)
    weights_first()
    for h in range(C):
        loads[C + h].wait()
    for dc in range(C - 1, -1, -1):
        loop(0, nb, lambda i: scatter(i, dot(wt0[i], x_v[half(dc), rows_at(i), :])), 8)
        pack(ONE, dc)
        launch(ONE, dc, range(Q))
        near(ONE, dc)
    for dc in range(C - 1, -1, -1):
        launch(COT, dc, late)
    forward(1, 1, 2)
    pair(3)
    forward(1, 2)
    forward(2, 1, 2)
    gather(1)
    forward(2, 2)
    weights(1)
    for q in early:
        arrive(COT, q)
    swap(B4)

    def first(q):
        arrive(ONE, q)
        base = chunk(q) * (NBT // Q)
        loop(0, NBT // Q, lambda n: stored(sf1, base + n, dot(weight(wt, 1, base + n), block(ONE, base + n))), 8)

    forward(3, 1, 2)
    gather(2)
    forward(3, 2)
    weights(2)
    for q in early:
        first(q)
    swap(M1)
    for q in late:
        first(q)

    def bent(i):
        v = gathered(sf1, i, PITCH, NBT).astype(BF16).astype(F32)
        square = v * v
        return v, square, jnp.tanh(C0 * (v + C1 * (square * v)))

    def middle(p, side):
        i = lax.rem(s0 + p, NBT)
        v, _, t = bent(i)
        hidden = (v * (0.5 * (1.0 + t))).astype(BF16)
        if side:
            op[HID, rows_at(p), :] = hidden
        stored(sf2, i, dot(weight(wt, 2, i), hidden))

    def slopes(i):
        v, square, t = bent(i)
        slope = 0.5 * (1.0 + t) + 0.5 * v * (1.0 - t * t) * (C0 * (1.0 + 3.0 * C1 * square))
        if tiled:
            stored(slp, i, slope)
        else:
            for u in range(U):
                sf1[pl.ds(u * NBT + i, NBT, stride=PITCH), :] = slope[u * NBT:(u + 1) * NBT]

    loop(0, SB, lambda p: middle(p, True), 8)
    swap(HID)
    loop(SB, NBT, lambda p: middle(p, False), 8)
    take_side(M2, sf2)
    swap(M2)
    gather(3)
    loop(0, NBT // 2, slopes, 8)
    loads[2 * C].wait()
    inverses = {}
    swapped(M2)
    swapped(B4)
    inverses[3] = gradient(3, ops(M2), ops(B4))
    loop(NBT // 2, NBT, slopes, 8)
    landed(3)

    def collect(k):
        for dc in range(C - 1, -1, -1):
            def one(n, dc=dc):
                value = gathered(sl, half(dc) * nb + n, SLP, SB)
                od[k - D1, dc, rows_at(n), :] = value.astype(BF16)

            loop(0, nb, one, 8)
            if dc:
                o_copy(k, dc).start()

    def fourth(p, side):
        j = lax.rem(s0 + p, NBT)
        two = taken(M2, sf2, p, j, side)
        sl[pl.ds(pl.multiple_of(j * SLP, 8), U * SB), :] = dot(side_weight(wt, 3, j), two)

    def last_forward(polls):
        if tiled:
            polls[0]()
        loop(0, SB, lambda p: fourth(p, True), 8)
        if tiled:
            polls[1]()
        loop(SB, NBT, lambda p: fourth(p, False), 8)
        if tiled:
            polls[2]()
        collect(LAST)

    if not tiled:
        flip(3)
        last_forward(())

    def third_back(q):
        base = chunk(q) * (NBT // Q)
        loop(0, NBT // Q, lambda n: stored(sb3, base + n, dot(weight(wn, 3, base + n), block(COT, base + n))), 8)

    for q in early:
        third_back(q)
    if tiled:
        flip(3)
    for q in late:
        arrive(COT, q)
        third_back(q)
    take_side(D3, sb3)
    swap(D3)
    combine(3)

    def second_back(p, side):
        i = lax.rem(s0 + p, NBT)
        slope = slp[pl.ds(pl.multiple_of(i * PITCH, 8), B), :] if tiled else gathered(sf1, i, PITCH, NBT)
        stored(sb2, i, dot(weight(wn, 2, i), taken(D3, sb3, p, i, side)) * slope)

    loop(0, SB, lambda p: second_back(p, True), 8)
    swapped(HID)
    swapped(D3)
    inverses[2] = gradient(2, ops(HID), ops(D3))
    loop(SB, NBT, lambda p: second_back(p, False), 8)
    take_side(D2, sb2)
    swap(D2)

    def first_back(p, side):
        j = lax.rem(s0 + p, NBT)
        sl[pl.ds(pl.multiple_of(j * SLP, 8), U * SB), :] = dot(side_weight(wn, 1, j), taken(D2, sb2, p, j, side))

    loop(0, SB, lambda p: first_back(p, True), 8)
    loop(SB, NBT, lambda p: first_back(p, False), 8)
    collect(D1)
    swapped(M1)
    swapped(D2)
    inverses[1] = gradient(1, ops(M1), ops(D2))
    combine(2)
    swapped(D1)
    inverses[0] = gradient(0, lambda dc, n: x_v[back(dc), rows_at(n), :], ops(D1))
    if tiled:
        last_forward((
            lambda: combine(1),
            lambda: combine(0, 1, 2, False),
            lambda: combine(0, 2, half_group - 1, False),
        ))
        combine(0, half_group - 1, None, False)
    else:
        combine(1)
    stores = []

    def save(ref, value_ref, h, sem):
        to = pl.ds(pl.multiple_of(h * LANES, LANES), LANES)
        stores.append(pltpu.make_async_copy(value_ref, ref.at[:, to], sem))
        stores[-1].start()

    for dc in range(C):
        def last_back(n, dc=dc):
            h = back(dc)
            value = c_v[h, rows_at(n), :].astype(F32) + dot(wn0[n], op_rows(D1, dc, n))
            c_v[h, rows_at(n), :] = value.astype(BF16)

        loop(0, nb, last_back, 8)
        save(igrad, c_v.at[back(dc)], back(dc), st.at[2 * F + dc])
    if tiled:
        combine(0, half_group)
    else:
        combine(0)

    def mean(f):
        loop(1, half_group, lambda d: c_copy(f, d).wait_recv())

        def column(s):
            col = pl.ds(pl.multiple_of(s * B, B), B)
            total = crx[f, 0, :, col].astype(F32)
            for g in range(1, half_group):
                total = total + crx[f, g, :, col].astype(F32)
            m_v[f, :, col] = total * inverses[f] / G

        loop(0, CS, column)
        stores.append(pltpu.make_async_copy(m_v.at[f], gmean.at[f], st.at[F + f]))
        stores[-1].start()

    swapped(LAST)
    for dc in range(C):
        ref = ox.at[LAST, dc - 1] if dc else od.at[LAST - D1, 0]

        def finish(n, dc=dc, ref=ref):
            value = x_v[back(dc), rows_at(n), :].astype(F32) + ref[rows_at(n), :].astype(F32)
            ref[rows_at(n), :] = value.astype(BF16)

        loop(0, nb, finish, 8)
        save(out, ref, back(dc), st.at[2 * F + C + dc])
    for f in (3, 2, 1, 0):
        mean(f)
    for f in range(F):
        pltpu.make_async_copy(e_v.at[f], nerr.at[0, f], st.at[f]).wait()
    for cp in stores:
        cp.wait()

    def handed(d):
        for f in range(F):
            if not line:
                w_copy(f, d).wait_send()
            q_copy(f, d).wait_send()
            c_copy(f, d).wait_send()
            p_copy(f, d, from_z(d)).wait_send()

    steps(1, half_group, handed)
    if line:
        for f in range(F):
            hop(f, dev, pair_z, 1, 1).wait_send()

        @pl.when(inner)
        def _():
            for f in range(F):
                hop(f, dev, 3 - z, 2, 2).wait_send()
                for copy in hops(f):
                    copy().wait_send()
    for f in range(F):
        p_copy(f, 0, dev).wait_send()
        q_copy(f, 0).wait_send()
    for f in range(1, F):
        for dy in range(1, Y):
            y_copy(f, dy).wait_send()
        for dc in range(1, C):
            loop(0, G, lambda n: k_copy(f, dc, n, dev).wait_send())
    for k in range(8):
        for dc in range(1, C):
            o_copy(k, dc).wait_send()
    for k in (COT, ONE):
        for dy in range(Y):
            for dc in range(C):
                if dy or dc:
                    for q in range(Q):
                        x_copy(k, dy, dc, q).wait_send()


def step(G, M, inp, cot, fac, expo, err):
    F, nb, S = fac.shape
    R, T = inp.shape
    C = T // LANES
    Y = M // C
    NBT = M * nb
    U = B // NBT
    SB = C * nb
    tiled = (S // B) % 16 == 0
    hbm = pl.BlockSpec(memory_space=pl.ANY)
    dma = pltpu.SemaphoreType.DMA
    return pl.pallas_call(
        functools.partial(kernel, G, M),
        out_shape=(
            jax.ShapeDtypeStruct((R, T), BF16),
            jax.ShapeDtypeStruct((R, T), BF16),
            jax.ShapeDtypeStruct(fac.shape, F32),
            jax.ShapeDtypeStruct(err.shape, BF16),
        ),
        in_specs=[hbm, hbm, hbm, pl.BlockSpec(memory_space=pltpu.SMEM), hbm],
        out_specs=(hbm,) * 4,
        scratch_shapes=[
            pltpu.VMEM((C, R, LANES), BF16),
            pltpu.VMEM((C, R, LANES), BF16),
            pltpu.VMEM((F, nb, B * B), BF16),
            pltpu.VMEM((max(NBT * (U * nb + PAD), B * (nb + PAD)), LANES), F32),
            pltpu.VMEM((2, C, NBT * U, nb, LANES), BF16),
            pltpu.VMEM((2, NBT * U, NBT, LANES), BF16),
            pltpu.VMEM((NBT * (B + PAD), LANES), F32),
            pltpu.VMEM((NBT * (B + PAD), LANES), F32),
            pltpu.VMEM((NBT * (B + PAD), LANES), F32),
            pltpu.VMEM((NBT * (B + PAD) if tiled else B, LANES), F32),
            pltpu.VMEM((NBT * (U * SB + PAD), LANES), F32),
            pltpu.VMEM((4, SB * B, LANES), BF16),
            pltpu.VMEM((8, C - 1, R, LANES), BF16),
            pltpu.VMEM((2, C, R, LANES), BF16),
            pltpu.VMEM((F, nb, S), BF16),
            pltpu.VMEM((1, nb, S) if tiled else (G, nb, S), BF16),
            pltpu.VMEM((1, 1, 1, 1, nb, S) if tiled else (F - 1, G, C, Y, nb, S), BF16),
            pltpu.VMEM((nb, B, B), BF16),
            pltpu.VMEM((nb, B, B), BF16),
            pltpu.VMEM((F - 1, Y, C, nb, B, B), BF16),
            pltpu.VMEM((F - 1, Y, C, nb, B, B), BF16),
            pltpu.VMEM((F, G, nb, S), BF16),
            pltpu.VMEM((F, G, nb, S), BF16),
            pltpu.VMEM((F, nb, S), F32),
            dma((2 * C + 1 + F,)),
            dma((2 * F + 2 * C,)),
            dma((2, M, Q)),
            dma((2, M, Q)),
            dma((F, Y)),
            dma((F, Y)),
            dma((F, max(G // 2, 6))),
            dma((F, G // 2)),
            dma((F, G // 2)),
            dma((F, G // 2)),
            dma((F, C, G)),
            dma((F, C, G)),
            dma((8, C)),
            dma((8, C)),
            dma((F, G // 2)),
            dma((F, G // 2)),
            dma((F, G // 2)),
            dma((F, G // 2)),
        ],
        compiler_params=pltpu.CompilerParams(
            collective_id=0, has_side_effects=True, vmem_limit_bytes=62 * 1024 * 1024
        ),
    )(inp, cot, fac, expo, err)


def solution(mesh):
    G, M = mesh.shape["dev"], mesh.shape["ma"]
    in_specs = (
        P("ma", "dev"),
        P("ma", "dev"),
        P(None, "ma", "dev"),
        P(None, "ma"),
        P("dev", None, "ma", None),
    )
    out_specs = (P("ma", "dev"), P("ma", "dev"), P(None, "ma", "dev"), P("dev", None, "ma", None))
    return jax.shard_map(
        functools.partial(step, G, M), mesh=mesh, in_specs=in_specs, out_specs=out_specs, check_vma=False
    )
```

```python
import functools

import jax
import jax.numpy as jnp
from jax import lax
from jax.experimental import pallas as pl
from jax.experimental.pallas import tpu as pltpu
from jax.sharding import PartitionSpec as P

B = 128
LANES = 128
PAD = 8
Q = 4
LIMIT = 127.0
C0 = 0.7978845608028654
C1 = 0.044715
F32 = jnp.float32
BF16 = jnp.bfloat16
MESH = pl.DeviceIdType.MESH
COT, ONE = range(2)
HID, D3, M2, D2, B4, M1, D1, LAST = range(8)


def dot(a, b):
    return lax.dot_general(a, b, (((1,), (0,)), ((), ())), preferred_element_type=F32)


def dot_nt(a, b):
    return lax.dot_general(a, b, (((1,), (1,)), ((), ())), preferred_element_type=F32)


def kernel(
    G, M, inp, cot, fac, expo, err, out, igrad, gmean, nerr,
    x_v, c_v, e_v, gs, tx, rx, sf1, sf2, sb3, slp, sl, op, ox, od, fv, wg0, wg, wn0, wt0, wn, wt, cod, crx, m_v,
    ld, st, xs, xr, ys, yr, ws, wr, ps, pr, ks, kr, os, orr, cs_s, cs_r, qs, qr,
):
    F, nb, S = fac.shape
    C = x_v.shape[0]
    Y = M // C
    NBT = M * nb
    U = B // NBT
    CS = S // B
    SB = C * nb
    PITCH = B + PAD
    SLP = U * SB + PAD
    XP = U * nb + PAD
    GP = nb + PAD
    JR = NBT * U // Q
    tiled = CS % 16 == 0
    ma = lax.axis_index("ma")
    dev = lax.axis_index("dev")
    y, c = ma // C, lax.rem(ma, C)
    s0 = y * SB
    sb2 = sf1 if tiled else sf2
    half_group = G // 2
    partner = dev + 1 - 2 * lax.rem(dev, 2)
    line = half_group == 4
    z, x = dev // 2, lax.rem(dev, 2)
    low = z // 2
    pair_z = z + 1 - 2 * lax.rem(z, 2)
    inner = jnp.logical_or(z == 1, z == 2)

    def lanes(h):
        return slice(h * LANES, (h + 1) * LANES)

    def half(dc):
        return lax.rem(c + dc, C)

    def back(dc):
        return lax.rem(c + C - dc, C)

    def at(dy, dc):
        return {"ma": lax.rem(y + dy, Y) * C + lax.rem(c + dc, C)}

    def loop(lo, hi, fn, unroll=1):
        def one(i, _):
            fn(i)
            return 0

        lax.fori_loop(lo, hi, one, 0, unroll=unroll)

    def steps(lo, hi, fn):
        if line:
            for d in range(lo, hi):
                fn(d)
        else:
            loop(lo, hi, fn)

    loads = []
    for h in range(C):
        loads.append(pltpu.make_async_copy(cot.at[:, lanes(h)], c_v.at[h], ld.at[h]))
    for h in range(C):
        loads.append(pltpu.make_async_copy(inp.at[:, lanes(h)], x_v.at[h], ld.at[C + h]))
    loads.append(pltpu.make_async_copy(err.at[0], e_v, ld.at[2 * C]))
    if tiled:
        own = [pltpu.make_async_copy(fac, fv, ld.at[2 * C + 1])]
    else:
        own = [pltpu.make_async_copy(fac.at[0], wg0.at[dev], ld.at[2 * C + 1])]
        for f in range(1, F):
            own.append(pltpu.make_async_copy(fac.at[f], wg.at[f - 1, dev, c, y], ld.at[2 * C + 1 + f]))
    for cp in own:
        cp.start()
    for cp in loads:
        cp.start()

    barrier = pltpu.get_barrier_semaphore()
    for d in range(1, M):
        pl.semaphore_signal(barrier, inc=1, device_id={"ma": lax.rem(ma + d, M)}, device_id_type=MESH)

    def greet(d):
        pl.semaphore_signal(barrier, inc=1, device_id={"dev": lax.rem(dev + d, G)}, device_id_type=MESH)

    loop(1, G, greet)

    def remote(src, dst, send, recv, to):
        return pltpu.make_async_remote_copy(
            src_ref=src, dst_ref=dst, send_sem=send, recv_sem=recv, device_id=to, device_id_type=MESH
        )

    def slot_of(f, g):
        if tiled:
            rows = pl.ds(pl.multiple_of(g * CS, CS), CS)
            return wn0.at[:, rows, :] if f == 0 else wn.at[f - 1, :, c, :, rows, :]
        return wg0.at[g] if f == 0 else wg.at[f - 1, g, c]

    def mine(f):
        if tiled:
            return wn.at[f - 1, y, c, :, pl.ds(pl.multiple_of(dev * CS, CS), CS), :]
        return wg.at[f - 1, dev, c, y]

    def y_copy(f, dy):
        return remote(mine(f), mine(f), ys.at[f, dy], yr.at[f, dy], at(dy, 0))

    def w_copy(f, d):
        return remote(slot_of(f, dev), slot_of(f, dev), ws.at[f, d], wr.at[f, d], {"dev": lax.rem(dev + 2 * d, G)})

    def hop(f, slot, to_z, sent, d):
        return remote(slot_of(f, slot), slot_of(f, slot), ws.at[f, sent], wr.at[f, d], {"dev": to_z * 2 + x})

    def hops(f):
        return [
            functools.partial(hop, f, from_z(1), 3 - z, 3, 3),
            functools.partial(hop, f, from_z(2), pair_z, 4, 2),
            functools.partial(hop, f, from_z(3), pair_z, 5, 3),
        ]

    def p_copy(f, d, slot):
        return remote(slot_of(f, slot), slot_of(f, slot), ps.at[f, d], pr.at[f, d], {"dev": partner})

    def k_copy(f, dc, n, slot):
        return remote(slot_of(f, slot), slot_of(f, slot), ks.at[f, dc, n], kr.at[f, dc, n], at(0, dc))

    def place(d):
        if d == 0:
            return z
        if d == 1:
            return pair_z
        return (2 - low) if d == 2 else (3 - 3 * low)

    def from_z(d):
        return place(d) * 2 + x if line else lax.rem(dev + G - 2 * d, G)

    def from_x(d):
        return place(d) * 2 + 1 - x if line else lax.rem(partner + G - 2 * d, G)

    def spread_on(f, n, slot):
        if f:
            for dc in range(1, C):
                k_copy(f, dc, n, slot).start()

    def forward(f, lo=1, hi=None):
        def one(d):
            w_copy(f, d).wait_recv()
            if line:
                @pl.when(inner)
                def _():
                    hops(f)[d - 1]().start()
            p_copy(f, d, from_z(d)).start()
            spread_on(f, d, from_z(d))

        steps(lo, half_group if hi is None else hi, one)

    def gather(f):
        def one(d):
            p_copy(f, d, from_x(d)).wait_recv()
            spread_on(f, half_group + d, from_x(d))

        steps(0, half_group, one)

    def push(f):
        if f:
            for dy in range(1, Y):
                y_copy(f, dy).wait_recv()
        if line:
            hop(f, dev, pair_z, 1, 1).start()

            @pl.when(inner)
            def _():
                hop(f, dev, 3 - z, 2, 2).start()
        else:
            loop(1, half_group, lambda d: w_copy(f, d).start())

    def pair(f):
        p_copy(f, 0, dev).start()
        spread_on(f, 0, dev)

    def x_copy(k, dy, dc, q):
        jq = lax.rem(lax.rem(y + dy, Y) * (Q // Y) + q, Q)
        rows = pl.ds(pl.multiple_of(jq * JR, JR), JR)
        return remote(
            tx.at[k, dc, rows], rx.at[k, rows, pl.ds(pl.multiple_of(ma * nb, nb), nb), :],
            xs.at[k, dy * C + dc, q], xr.at[k, dy * C + dc, q], at(dy, dc),
        )

    def chunk(q):
        return lax.rem(y * (Q // Y) + q, Q)

    def arrive(k, q):
        for dy in range(Y):
            for dc in range(C):
                if dy or dc:
                    x_copy(k, dy, dc, q).wait_recv()

    def launch(k, dc, qs_):
        for q in qs_:
            for dy in range(1, Y):
                x_copy(k, dy, dc, q).start()

    def near(k, dc):
        if dc:
            for q in range(Q):
                x_copy(k, 0, dc, q).start()

    def o_copy(k, dc):
        blocks = half(dc) * nb
        if k < B4:
            src = op.at[k, pl.ds(pl.multiple_of(blocks * B, B), nb * B), :]
        elif k < D1:
            src = rx.at[COT if k == B4 else ONE, pl.ds(pl.multiple_of((s0 + blocks) * U, U), nb * U)]
        else:
            src = od.at[k - D1, dc]
        dst = ox.at[k, dc - 1]
        if B4 <= k < D1:
            dst = dst.reshape(nb * U, NBT, LANES)
        return remote(src, dst, os.at[k, dc], orr.at[k, dc], at(0, dc))

    def swap(k):
        for dc in range(1, C):
            o_copy(k, dc).start()

    def swapped(k):
        for dc in range(1, C):
            o_copy(k, dc).wait_recv()

    def q_copy(f, d):
        return remote(cod.at[f, d], crx.at[f, half_group + d], qs.at[f, d], qr.at[f, d], {"dev": partner})

    def c_copy(f, d):
        return remote(
            cod.at[f, half_group + d], crx.at[f, d], cs_s.at[f, d], cs_r.at[f, d], {"dev": lax.rem(dev + 2 * d, G)}
        )

    def combine(f, lo=1, hi=None, ending=True):
        def one(d):
            q_copy(f, d).wait_recv()
            both = cod[f, half_group + d].astype(F32) + crx[f, half_group + d].astype(F32)
            cod[f, half_group + d] = both.astype(BF16)
            c_copy(f, d).start()

        loop(lo, half_group if hi is None else hi, one)
        if ending:
            q_copy(f, 0).wait_recv()
            crx[f, 0] = (cod[f, half_group].astype(F32) + crx[f, half_group].astype(F32)).astype(BF16)

    def scatter(i, value):
        for u in range(U):
            gs[pl.ds(u * nb + i, NBT, stride=XP), :] = value[u * NBT:(u + 1) * NBT]

    def pack(k, dc):
        def one(j):
            rows = gs[pl.ds(pl.multiple_of(j * XP, 8), U * nb), :]
            value = rows.astype(BF16).reshape(U, nb, LANES)
            to = pl.ds(pl.multiple_of(j * U, U), U)
            tx[k, dc, to] = value
            if dc == 0:
                rx[k, to, pl.ds(pl.multiple_of(ma * nb, nb), nb), :] = value

        loop(0, NBT, one, 8)

    def rows_at(n):
        return pl.ds(pl.multiple_of(n * B, B), B)

    def block(k, j):
        return rx[k, pl.ds(j * U, U)].reshape(B, LANES)

    def gathered(ref, i, pitch, step):
        return jnp.concatenate([ref[pl.ds(u * step + i, NBT, stride=pitch), :] for u in range(U)], axis=0)

    def stored(ref, j, value):
        ref[pl.ds(pl.multiple_of(j * PITCH, 8), B), :] = value

    def take_side(k, ref):
        def one(p):
            op[k, rows_at(p), :] = gathered(ref, s0 + p, PITCH, NBT).astype(BF16)

        loop(0, SB, one, 8)

    def taken(k, ref, p, i, side):
        return op[k, rows_at(p), :] if side else gathered(ref, i, PITCH, NBT).astype(BF16)

    def widen(piece):
        def one(g):
            for s in range(CS):
                to = pl.multiple_of((g * CS + s) * GP, 8)
                gs[pl.ds(to, nb), :] = piece(g, s)

        loop(0, G, one)

    def arrange():
        for cp in own:
            cp.wait()
        if tiled:
            for f in range(F):
                for s in range(CS):
                    gs[(f * CS + s) * GP:(f * CS + s) * GP + nb, :] = fv[f, :, s * B:(s + 1) * B].astype(F32)
            for f in range(F):
                def one(n, f=f):
                    tile = gs[pl.ds(f * CS * GP + n, CS, stride=GP), :].astype(BF16)
                    rows = pl.ds(pl.multiple_of(dev * CS, CS), CS)
                    if f:
                        wn[f - 1, y, c, n, rows, :] = tile
                    else:
                        wn0[n, rows, :] = tile

                loop(0, nb, one, 4)

    def weights_first():
        if not tiled:
            widen(lambda g, s: wg0[g, :, s * B:(s + 1) * B].astype(F32))

        def take(n):
            if not tiled:
                wn0[n] = gs[pl.ds(n, B, stride=GP), :].astype(BF16)
            wt0[n] = wn0[n].T

        loop(0, nb, take, 8)

    def landed(f):
        for dc in range(1, C):
            def came(n, dc=dc):
                k_copy(f, dc, n, dev).wait_recv()

            loop(0, G, came)

    def flip(f):
        def group(m):
            yy, cc = m // C, lax.rem(m, C)
            if not tiled:
                widen(lambda g, s: wg[f - 1, g, cc, yy, :, s * B:(s + 1) * B].astype(F32))

            def take(n):
                if not tiled:
                    wn[f - 1, yy, cc, n] = gs[pl.ds(n, B, stride=GP), :].astype(BF16)
                wt[f - 1, yy, cc, n] = wn[f - 1, yy, cc, n].T

            loop(0, nb, take, 8)

        loop(0, M, group)

    def weights(f):
        landed(f)
        flip(f)

    def weight(ref, f, j):
        return ref[f - 1, j // SB, lax.rem(j, SB) // nb, lax.rem(j, nb)]

    def side_weight(ref, f, j):
        at_j = ref.at[f - 1, j // SB, lax.rem(j, SB) // nb, lax.rem(j, nb)]
        rows = [at_j[pl.ds(pl.multiple_of(u * NBT + s0, nb), SB), :] for u in range(U)]
        return jnp.concatenate(rows, axis=0)

    def gradient(f, left, right):
        def one(n):
            a = jnp.concatenate([left(dc, n) for dc in range(C)], axis=1)
            b = jnp.concatenate([right(dc, n) for dc in range(C)], axis=1)
            gs[pl.ds(n, B, stride=GP), :] = dot_nt(a, b)

        loop(0, nb, one, 16)
        row = lax.broadcasted_iota(jnp.int32, (nb, B), 0)
        power = jnp.zeros((nb, B), jnp.int32)
        for n in range(nb):
            power = jnp.where(row == n, expo[f, n], power)
        scale = jnp.left_shift(jnp.ones_like(power), -power).astype(F32)
        inverse = jnp.left_shift(jnp.ones_like(power), 24 + power).astype(F32) * (2.0 ** -24)

        def quantize(g, slot):
            for s in range(CS):
                col = pl.ds(pl.multiple_of((g * CS + s) * B, B), B)
                total = gs[pl.ds(pl.multiple_of((g * CS + s) * GP, 8), nb), :] + e_v[f, :, col].astype(F32)
                code = jnp.clip(total * scale, -LIMIT, LIMIT)
                e_v[f, :, col] = (total - code * inverse).astype(BF16)
                cod[f, slot, :, s * B:(s + 1) * B] = code.astype(BF16)

        def away(step):
            d = lax.rem(step + 1, half_group)
            quantize(lax.rem(partner + 2 * d, G), d)
            q_copy(f, d).start()

        loop(0, half_group, away)
        loop(0, half_group, lambda d: quantize(lax.rem(dev + 2 * d, G), half_group + d))
        pltpu.make_async_copy(e_v.at[f], nerr.at[0, f], st.at[f]).start()
        return inverse

    def op_rows(k, dc, n):
        if dc:
            return ox[k, dc - 1, rows_at(n), :]
        if k < B4:
            return op[k, rows_at(c * nb + n), :]
        if k < D1:
            return block(COT if k == B4 else ONE, ma * nb + n)
        return od[k - D1, 0, rows_at(n), :]

    def ops(k):
        return functools.partial(op_rows, k)

    def spread_cot(dc):
        loop(0, nb, lambda i: scatter(i, c_v[half(dc), rows_at(i), :].astype(F32)), 8)
        pack(COT, dc)

    early, late = tuple(range(Q // Y)), tuple(range(Q // Y, Q))
    arrange()
    pl.semaphore_wait(barrier, M - 1 + G - 1)
    push(0)
    pair(0)
    for f in range(1, F):
        for dy in range(1, Y):
            y_copy(f, dy).start()
    for h in range(C):
        loads[h].wait()
    for dc in range(C - 1, -1, -1):
        spread_cot(dc)
        launch(COT, dc, early)
        near(COT, dc)

    forward(0, 1, 2)
    push(1)
    pair(1)
    forward(0, 2)
    push(2)
    push(3)
    pair(2)
    gather(0)
    weights_first()
    for h in range(C):
        loads[C + h].wait()
    for dc in range(C - 1, -1, -1):
        loop(0, nb, lambda i: scatter(i, dot(wt0[i], x_v[half(dc), rows_at(i), :])), 8)
        pack(ONE, dc)
        near(ONE, dc)
    for k, some in ((ONE, range(Q)), (COT, late)):
        for q in some:
            for dc in range(C - 1, -1, -1):
                launch(k, dc, (q,))
    forward(1, 1, 2)
    pair(3)
    forward(1, 2)
    forward(2, 1, 2)
    gather(1)
    forward(2, 2)
    weights(1)
    for q in early:
        arrive(COT, q)
    swap(B4)

    def first(q):
        arrive(ONE, q)
        base = chunk(q) * (NBT // Q)
        loop(0, NBT // Q, lambda n: stored(sf1, base + n, dot(weight(wt, 1, base + n), block(ONE, base + n))), 8)

    forward(3, 1, 2)
    gather(2)
    forward(3, 2)
    weights(2)
    for q in early:
        first(q)
    swap(M1)
    for q in late:
        first(q)

    def bent(i):
        v = gathered(sf1, i, PITCH, NBT).astype(BF16).astype(F32)
        square = v * v
        return v, square, jnp.tanh(C0 * (v + C1 * (square * v)))

    def middle(p, side):
        i = lax.rem(s0 + p, NBT)
        v, _, t = bent(i)
        hidden = (v * (0.5 * (1.0 + t))).astype(BF16)
        if side:
            op[HID, rows_at(p), :] = hidden
        stored(sf2, i, dot(weight(wt, 2, i), hidden))

    def slopes(i):
        v, square, t = bent(i)
        slope = 0.5 * (1.0 + t) + 0.5 * v * (1.0 - t * t) * (C0 * (1.0 + 3.0 * C1 * square))
        if tiled:
            stored(slp, i, slope)
        else:
            for u in range(U):
                sf1[pl.ds(u * NBT + i, NBT, stride=PITCH), :] = slope[u * NBT:(u + 1) * NBT]

    loop(0, SB, lambda p: middle(p, True), 8)
    swap(HID)
    loop(SB, NBT, lambda p: middle(p, False), 8)
    take_side(M2, sf2)
    swap(M2)
    gather(3)
    loop(0, NBT // 2, slopes, 8)
    loads[2 * C].wait()
    inverses = {}
    swapped(M2)
    swapped(B4)
    inverses[3] = gradient(3, ops(M2), ops(B4))
    loop(NBT // 2, NBT, slopes, 8)
    landed(3)

    def collect(k):
        for dc in range(C - 1, -1, -1):
            def one(n, dc=dc):
                value = gathered(sl, half(dc) * nb + n, SLP, SB)
                od[k - D1, dc, rows_at(n), :] = value.astype(BF16)

            loop(0, nb, one, 8)
            if dc:
                o_copy(k, dc).start()

    def fourth(p, side):
        j = lax.rem(s0 + p, NBT)
        two = taken(M2, sf2, p, j, side)
        sl[pl.ds(pl.multiple_of(j * SLP, 8), U * SB), :] = dot(side_weight(wt, 3, j), two)

    def last_forward(polls):
        if tiled:
            polls[0]()
        loop(0, SB, lambda p: fourth(p, True), 8)
        if tiled:
            polls[1]()
        loop(SB, NBT, lambda p: fourth(p, False), 8)
        if tiled:
            polls[2]()
        collect(LAST)

    if not tiled:
        flip(3)
        last_forward(())

    def third_back(q):
        base = chunk(q) * (NBT // Q)
        loop(0, NBT // Q, lambda n: stored(sb3, base + n, dot(weight(wn, 3, base + n), block(COT, base + n))), 8)

    for q in early:
        third_back(q)
    if tiled:
        flip(3)
    for q in late:
        arrive(COT, q)
        third_back(q)
    take_side(D3, sb3)
    swap(D3)

    def second_back(p, side):
        i = lax.rem(s0 + p, NBT)
        slope = slp[pl.ds(pl.multiple_of(i * PITCH, 8), B), :] if tiled else gathered(sf1, i, PITCH, NBT)
        stored(sb2, i, dot(weight(wn, 2, i), taken(D3, sb3, p, i, side)) * slope)

    loop(0, SB, lambda p: second_back(p, True), 8)
    combine(3)
    loop(SB, NBT, lambda p: second_back(p, False), 8)
    take_side(D2, sb2)
    swap(D2)
    swapped(HID)
    swapped(D3)
    inverses[2] = gradient(2, ops(HID), ops(D3))

    def first_back(p, side):
        j = lax.rem(s0 + p, NBT)
        sl[pl.ds(pl.multiple_of(j * SLP, 8), U * SB), :] = dot(side_weight(wn, 1, j), taken(D2, sb2, p, j, side))

    loop(0, SB, lambda p: first_back(p, True), 8)
    loop(SB, NBT, lambda p: first_back(p, False), 8)
    collect(D1)
    swapped(M1)
    swapped(D2)
    inverses[1] = gradient(1, ops(M1), ops(D2))
    combine(2)
    swapped(D1)
    inverses[0] = gradient(0, lambda dc, n: x_v[back(dc), rows_at(n), :], ops(D1))
    if tiled:
        last_forward((
            lambda: combine(1),
            lambda: combine(0, 1, 2, False),
            lambda: combine(0, 2, half_group - 1, False),
        ))
        combine(0, half_group - 1, None, False)
    else:
        combine(1)
    stores = []

    def save(ref, value_ref, h, sem):
        to = pl.ds(pl.multiple_of(h * LANES, LANES), LANES)
        stores.append(pltpu.make_async_copy(value_ref, ref.at[:, to], sem))
        stores[-1].start()

    for dc in range(C):
        def last_back(n, dc=dc):
            h = back(dc)
            value = c_v[h, rows_at(n), :].astype(F32) + dot(wn0[n], op_rows(D1, dc, n))
            c_v[h, rows_at(n), :] = value.astype(BF16)

        loop(0, nb, last_back, 8)
        save(igrad, c_v.at[back(dc)], back(dc), st.at[2 * F + dc])
    if tiled:
        combine(0, half_group)
    else:
        combine(0)

    def mean(f):
        loop(1, half_group, lambda d: c_copy(f, d).wait_recv())

        def column(s):
            col = pl.ds(pl.multiple_of(s * B, B), B)
            total = crx[f, 0, :, col].astype(F32)
            for g in range(1, half_group):
                total = total + crx[f, g, :, col].astype(F32)
            m_v[f, :, col] = total * inverses[f] / G

        loop(0, CS, column)
        stores.append(pltpu.make_async_copy(m_v.at[f], gmean.at[f], st.at[F + f]))
        stores[-1].start()

    swapped(LAST)
    for dc in range(C):
        ref = ox.at[LAST, dc - 1] if dc else od.at[LAST - D1, 0]

        def finish(n, dc=dc, ref=ref):
            value = x_v[back(dc), rows_at(n), :].astype(F32) + ref[rows_at(n), :].astype(F32)
            ref[rows_at(n), :] = value.astype(BF16)

        loop(0, nb, finish, 8)
        save(out, ref, back(dc), st.at[2 * F + C + dc])
    for f in (3, 2, 1, 0):
        mean(f)
    for f in range(F):
        pltpu.make_async_copy(e_v.at[f], nerr.at[0, f], st.at[f]).wait()
    for cp in stores:
        cp.wait()

    def handed(d):
        for f in range(F):
            if not line:
                w_copy(f, d).wait_send()
            q_copy(f, d).wait_send()
            c_copy(f, d).wait_send()
            p_copy(f, d, from_z(d)).wait_send()

    steps(1, half_group, handed)
    if line:
        for f in range(F):
            hop(f, dev, pair_z, 1, 1).wait_send()

        @pl.when(inner)
        def _():
            for f in range(F):
                hop(f, dev, 3 - z, 2, 2).wait_send()
                for copy in hops(f):
                    copy().wait_send()
    for f in range(F):
        p_copy(f, 0, dev).wait_send()
        q_copy(f, 0).wait_send()
    for f in range(1, F):
        for dy in range(1, Y):
            y_copy(f, dy).wait_send()
        for dc in range(1, C):
            loop(0, G, lambda n: k_copy(f, dc, n, dev).wait_send())
    for k in range(8):
        for dc in range(1, C):
            o_copy(k, dc).wait_send()
    for k in (COT, ONE):
        for dy in range(Y):
            for dc in range(C):
                if dy or dc:
                    for q in range(Q):
                        x_copy(k, dy, dc, q).wait_send()


def step(G, M, inp, cot, fac, expo, err):
    F, nb, S = fac.shape
    R, T = inp.shape
    C = T // LANES
    Y = M // C
    NBT = M * nb
    U = B // NBT
    SB = C * nb
    tiled = (S // B) % 16 == 0
    hbm = pl.BlockSpec(memory_space=pl.ANY)
    dma = pltpu.SemaphoreType.DMA
    return pl.pallas_call(
        functools.partial(kernel, G, M),
        out_shape=(
            jax.ShapeDtypeStruct((R, T), BF16),
            jax.ShapeDtypeStruct((R, T), BF16),
            jax.ShapeDtypeStruct(fac.shape, F32),
            jax.ShapeDtypeStruct(err.shape, BF16),
        ),
        in_specs=[hbm, hbm, hbm, pl.BlockSpec(memory_space=pltpu.SMEM), hbm],
        out_specs=(hbm,) * 4,
        scratch_shapes=[
            pltpu.VMEM((C, R, LANES), BF16),
            pltpu.VMEM((C, R, LANES), BF16),
            pltpu.VMEM((F, nb, B * B), BF16),
            pltpu.VMEM((max(NBT * (U * nb + PAD), B * (nb + PAD)), LANES), F32),
            pltpu.VMEM((2, C, NBT * U, nb, LANES), BF16),
            pltpu.VMEM((2, NBT * U, NBT, LANES), BF16),
            pltpu.VMEM((NBT * (B + PAD), LANES), F32),
            pltpu.VMEM((NBT * (B + PAD), LANES), F32),
            pltpu.VMEM((NBT * (B + PAD), LANES), F32),
            pltpu.VMEM((NBT * (B + PAD) if tiled else B, LANES), F32),
            pltpu.VMEM((NBT * (U * SB + PAD), LANES), F32),
            pltpu.VMEM((4, SB * B, LANES), BF16),
            pltpu.VMEM((8, C - 1, R, LANES), BF16),
            pltpu.VMEM((2, C, R, LANES), BF16),
            pltpu.VMEM((F, nb, S), BF16),
            pltpu.VMEM((1, nb, S) if tiled else (G, nb, S), BF16),
            pltpu.VMEM((1, 1, 1, 1, nb, S) if tiled else (F - 1, G, C, Y, nb, S), BF16),
            pltpu.VMEM((nb, B, B), BF16),
            pltpu.VMEM((nb, B, B), BF16),
            pltpu.VMEM((F - 1, Y, C, nb, B, B), BF16),
            pltpu.VMEM((F - 1, Y, C, nb, B, B), BF16),
            pltpu.VMEM((F, G, nb, S), BF16),
            pltpu.VMEM((F, G, nb, S), BF16),
            pltpu.VMEM((F, nb, S), F32),
            dma((2 * C + 1 + F,)),
            dma((2 * F + 2 * C,)),
            dma((2, M, Q)),
            dma((2, M, Q)),
            dma((F, Y)),
            dma((F, Y)),
            dma((F, max(G // 2, 6))),
            dma((F, G // 2)),
            dma((F, G // 2)),
            dma((F, G // 2)),
            dma((F, C, G)),
            dma((F, C, G)),
            dma((8, C)),
            dma((8, C)),
            dma((F, G // 2)),
            dma((F, G // 2)),
            dma((F, G // 2)),
            dma((F, G // 2)),
        ],
        compiler_params=pltpu.CompilerParams(
            collective_id=0, has_side_effects=True, vmem_limit_bytes=62 * 1024 * 1024
        ),
    )(inp, cot, fac, expo, err)


def solution(mesh):
    G, M = mesh.shape["dev"], mesh.shape["ma"]
    in_specs = (
        P("ma", "dev"),
        P("ma", "dev"),
        P(None, "ma", "dev"),
        P(None, "ma"),
        P("dev", None, "ma", None),
    )
    out_specs = (P("ma", "dev"), P("ma", "dev"), P(None, "ma", "dev"), P("dev", None, "ma", None))
    return jax.shard_map(
        functools.partial(step, G, M), mesh=mesh, in_specs=in_specs, out_specs=out_specs, check_vma=False
    )
```

```python
import functools

import jax
import jax.numpy as jnp
from jax import lax
from jax.experimental import pallas as pl
from jax.experimental.pallas import tpu as pltpu
from jax.sharding import PartitionSpec as P

B = 128
LANES = 128
PAD = 8
Q = 4
LIMIT = 127.0
C0 = 0.7978845608028654
C1 = 0.044715
F32 = jnp.float32
BF16 = jnp.bfloat16
MESH = pl.DeviceIdType.MESH
COT, ONE = range(2)
HID, D3, M2, D2, B4, M1, D1, LAST = range(8)


def dot(a, b):
    return lax.dot_general(a, b, (((1,), (0,)), ((), ())), preferred_element_type=F32)


def dot_nt(a, b):
    return lax.dot_general(a, b, (((1,), (1,)), ((), ())), preferred_element_type=F32)


def kernel(
    G, M, inp, cot, fac, expo, err, out, igrad, gmean, nerr,
    x_v, c_v, e_v, gs, tx, rx, sf1, sf2, sb3, slp, sl, op, ox, od, fv, wg0, wg, wn0, wt0, wn, wt, cod, crx, m_v,
    ld, st, xs, xr, ys, yr, ws, wr, ps, pr, ks, kr, os, orr, cs_s, cs_r, qs, qr,
):
    F, nb, S = fac.shape
    C = x_v.shape[0]
    Y = M // C
    NBT = M * nb
    U = B // NBT
    CS = S // B
    SB = C * nb
    PITCH = B + PAD
    SLP = U * SB + PAD
    XP = U * nb + PAD
    GP = nb + PAD
    JR = NBT * U // Q
    tiled = CS % 16 == 0
    ma = lax.axis_index("ma")
    dev = lax.axis_index("dev")
    y, c = ma // C, lax.rem(ma, C)
    s0 = y * SB
    sb2 = sf1 if tiled else sf2
    half_group = G // 2
    partner = dev + 1 - 2 * lax.rem(dev, 2)
    line = half_group == 4
    z, x = dev // 2, lax.rem(dev, 2)
    low = z // 2
    pair_z = z + 1 - 2 * lax.rem(z, 2)
    inner = jnp.logical_or(z == 1, z == 2)

    def lanes(h):
        return slice(h * LANES, (h + 1) * LANES)

    def half(dc):
        return lax.rem(c + dc, C)

    def back(dc):
        return lax.rem(c + C - dc, C)

    def at(dy, dc):
        return {"ma": lax.rem(y + dy, Y) * C + lax.rem(c + dc, C)}

    def loop(lo, hi, fn, unroll=1):
        def one(i, _):
            fn(i)
            return 0

        lax.fori_loop(lo, hi, one, 0, unroll=unroll)

    def steps(lo, hi, fn):
        if line:
            for d in range(lo, hi):
                fn(d)
        else:
            loop(lo, hi, fn)

    loads = []
    for h in range(C):
        loads.append(pltpu.make_async_copy(cot.at[:, lanes(h)], c_v.at[h], ld.at[h]))
    for h in range(C):
        loads.append(pltpu.make_async_copy(inp.at[:, lanes(h)], x_v.at[h], ld.at[C + h]))
    loads.append(pltpu.make_async_copy(err.at[0], e_v, ld.at[2 * C]))
    if tiled:
        own = [pltpu.make_async_copy(fac, fv, ld.at[2 * C + 1])]
    else:
        own = [pltpu.make_async_copy(fac.at[0], wg0.at[dev], ld.at[2 * C + 1])]
        for f in range(1, F):
            own.append(pltpu.make_async_copy(fac.at[f], wg.at[f - 1, dev, c, y], ld.at[2 * C + 1 + f]))
    for cp in own:
        cp.start()
    for cp in loads:
        cp.start()

    barrier = pltpu.get_barrier_semaphore()
    for d in range(1, M):
        pl.semaphore_signal(barrier, inc=1, device_id={"ma": lax.rem(ma + d, M)}, device_id_type=MESH)

    def greet(d):
        pl.semaphore_signal(barrier, inc=1, device_id={"dev": lax.rem(dev + d, G)}, device_id_type=MESH)

    loop(1, G, greet)

    def remote(src, dst, send, recv, to):
        return pltpu.make_async_remote_copy(
            src_ref=src, dst_ref=dst, send_sem=send, recv_sem=recv, device_id=to, device_id_type=MESH
        )

    def slot_of(f, g):
        if tiled:
            rows = pl.ds(pl.multiple_of(g * CS, CS), CS)
            return wn0.at[:, rows, :] if f == 0 else wn.at[f - 1, :, c, :, rows, :]
        return wg0.at[g] if f == 0 else wg.at[f - 1, g, c]

    def mine(f):
        if tiled:
            return wn.at[f - 1, y, c, :, pl.ds(pl.multiple_of(dev * CS, CS), CS), :]
        return wg.at[f - 1, dev, c, y]

    def y_copy(f, dy):
        return remote(mine(f), mine(f), ys.at[f, dy], yr.at[f, dy], at(dy, 0))

    def w_copy(f, d):
        return remote(slot_of(f, dev), slot_of(f, dev), ws.at[f, d], wr.at[f, d], {"dev": lax.rem(dev + 2 * d, G)})

    def hop(f, slot, to_z, sent, d):
        return remote(slot_of(f, slot), slot_of(f, slot), ws.at[f, sent], wr.at[f, d], {"dev": to_z * 2 + x})

    def hops(f):
        return [
            functools.partial(hop, f, from_z(1), 3 - z, 3, 3),
            functools.partial(hop, f, from_z(2), pair_z, 4, 2),
            functools.partial(hop, f, from_z(3), pair_z, 5, 3),
        ]

    def p_copy(f, d, slot):
        return remote(slot_of(f, slot), slot_of(f, slot), ps.at[f, d], pr.at[f, d], {"dev": partner})

    def k_copy(f, dc, n, slot):
        return remote(slot_of(f, slot), slot_of(f, slot), ks.at[f, dc, n], kr.at[f, dc, n], at(0, dc))

    def place(d):
        if d == 0:
            return z
        if d == 1:
            return pair_z
        return (2 - low) if d == 2 else (3 - 3 * low)

    def from_z(d):
        return place(d) * 2 + x if line else lax.rem(dev + G - 2 * d, G)

    def from_x(d):
        return place(d) * 2 + 1 - x if line else lax.rem(partner + G - 2 * d, G)

    def spread_on(f, n, slot):
        if f:
            for dc in range(1, C):
                k_copy(f, dc, n, slot).start()

    def forward(f, lo=1, hi=None):
        def one(d):
            w_copy(f, d).wait_recv()
            if line:
                @pl.when(inner)
                def _():
                    hops(f)[d - 1]().start()
            p_copy(f, d, from_z(d)).start()
            spread_on(f, d, from_z(d))

        steps(lo, half_group if hi is None else hi, one)

    def gather(f):
        def one(d):
            p_copy(f, d, from_x(d)).wait_recv()
            spread_on(f, half_group + d, from_x(d))

        steps(0, half_group, one)

    def push(f):
        if f:
            for dy in range(1, Y):
                y_copy(f, dy).wait_recv()
        if line:
            hop(f, dev, pair_z, 1, 1).start()

            @pl.when(inner)
            def _():
                hop(f, dev, 3 - z, 2, 2).start()
        else:
            loop(1, half_group, lambda d: w_copy(f, d).start())

    def pair(f):
        p_copy(f, 0, dev).start()
        spread_on(f, 0, dev)

    def x_copy(k, dy, dc, q):
        jq = lax.rem(lax.rem(y + dy, Y) * (Q // Y) + q, Q)
        rows = pl.ds(pl.multiple_of(jq * JR, JR), JR)
        return remote(
            tx.at[k, dc, rows], rx.at[k, rows, pl.ds(pl.multiple_of(ma * nb, nb), nb), :],
            xs.at[k, dy * C + dc, q], xr.at[k, dy * C + dc, q], at(dy, dc),
        )

    def chunk(q):
        return lax.rem(y * (Q // Y) + q, Q)

    def arrive(k, q):
        for dy in range(Y):
            for dc in range(C):
                if dy or dc:
                    x_copy(k, dy, dc, q).wait_recv()

    def launch(k, dc, qs_):
        for q in qs_:
            for dy in range(1, Y):
                x_copy(k, dy, dc, q).start()

    def near(k, dc):
        if dc:
            for q in range(Q):
                x_copy(k, 0, dc, q).start()

    def o_copy(k, dc):
        blocks = half(dc) * nb
        if k < B4:
            src = op.at[k, pl.ds(pl.multiple_of(blocks * B, B), nb * B), :]
        elif k < D1:
            src = rx.at[COT if k == B4 else ONE, pl.ds(pl.multiple_of((s0 + blocks) * U, U), nb * U)]
        else:
            src = od.at[k - D1, dc]
        dst = ox.at[k, dc - 1]
        if B4 <= k < D1:
            dst = dst.reshape(nb * U, NBT, LANES)
        return remote(src, dst, os.at[k, dc], orr.at[k, dc], at(0, dc))

    def swap(k):
        for dc in range(1, C):
            o_copy(k, dc).start()

    def swapped(k):
        for dc in range(1, C):
            o_copy(k, dc).wait_recv()

    def q_copy(f, d):
        return remote(cod.at[f, d], crx.at[f, half_group + d], qs.at[f, d], qr.at[f, d], {"dev": partner})

    def c_copy(f, d):
        return remote(
            cod.at[f, half_group + d], crx.at[f, d], cs_s.at[f, d], cs_r.at[f, d], {"dev": lax.rem(dev + 2 * d, G)}
        )

    def combine(f, lo=1, hi=None, ending=True):
        def one(d):
            q_copy(f, d).wait_recv()
            both = cod[f, half_group + d].astype(F32) + crx[f, half_group + d].astype(F32)
            cod[f, half_group + d] = both.astype(BF16)
            c_copy(f, d).start()

        loop(lo, half_group if hi is None else hi, one)
        if ending:
            q_copy(f, 0).wait_recv()
            crx[f, 0] = (cod[f, half_group].astype(F32) + crx[f, half_group].astype(F32)).astype(BF16)

    def scatter(i, value):
        for u in range(U):
            gs[pl.ds(u * nb + i, NBT, stride=XP), :] = value[u * NBT:(u + 1) * NBT]

    def pack(k, dc):
        def one(j):
            rows = gs[pl.ds(pl.multiple_of(j * XP, 8), U * nb), :]
            value = rows.astype(BF16).reshape(U, nb, LANES)
            to = pl.ds(pl.multiple_of(j * U, U), U)
            tx[k, dc, to] = value
            if dc == 0:
                rx[k, to, pl.ds(pl.multiple_of(ma * nb, nb), nb), :] = value

        loop(0, NBT, one, 8)

    def rows_at(n):
        return pl.ds(pl.multiple_of(n * B, B), B)

    def block(k, j):
        return rx[k, pl.ds(j * U, U)].reshape(B, LANES)

    def gathered(ref, i, pitch, step):
        return jnp.concatenate([ref[pl.ds(u * step + i, NBT, stride=pitch), :] for u in range(U)], axis=0)

    def stored(ref, j, value):
        ref[pl.ds(pl.multiple_of(j * PITCH, 8), B), :] = value

    def take_side(k, ref):
        def one(p):
            op[k, rows_at(p), :] = gathered(ref, s0 + p, PITCH, NBT).astype(BF16)

        loop(0, SB, one, 8)

    def taken(k, ref, p, i, side):
        return op[k, rows_at(p), :] if side else gathered(ref, i, PITCH, NBT).astype(BF16)

    def widen(piece):
        def one(g):
            for s in range(CS):
                to = pl.multiple_of((g * CS + s) * GP, 8)
                gs[pl.ds(to, nb), :] = piece(g, s)

        loop(0, G, one)

    def arrange():
        for cp in own:
            cp.wait()
        if tiled:
            for f in range(F):
                for s in range(CS):
                    gs[(f * CS + s) * GP:(f * CS + s) * GP + nb, :] = fv[f, :, s * B:(s + 1) * B].astype(F32)
            for f in range(F):
                def one(n, f=f):
                    tile = gs[pl.ds(f * CS * GP + n, CS, stride=GP), :].astype(BF16)
                    rows = pl.ds(pl.multiple_of(dev * CS, CS), CS)
                    if f:
                        wn[f - 1, y, c, n, rows, :] = tile
                    else:
                        wn0[n, rows, :] = tile

                loop(0, nb, one, 4)

    def weights_first():
        if not tiled:
            widen(lambda g, s: wg0[g, :, s * B:(s + 1) * B].astype(F32))

        def take(n):
            if not tiled:
                wn0[n] = gs[pl.ds(n, B, stride=GP), :].astype(BF16)
            wt0[n] = wn0[n].T

        loop(0, nb, take, 8)

    def landed(f):
        for dc in range(1, C):
            def came(n, dc=dc):
                k_copy(f, dc, n, dev).wait_recv()

            loop(0, G, came)

    def flip(f):
        def group(m):
            yy, cc = m // C, lax.rem(m, C)
            if not tiled:
                widen(lambda g, s: wg[f - 1, g, cc, yy, :, s * B:(s + 1) * B].astype(F32))

            def take(n):
                if not tiled:
                    wn[f - 1, yy, cc, n] = gs[pl.ds(n, B, stride=GP), :].astype(BF16)
                wt[f - 1, yy, cc, n] = wn[f - 1, yy, cc, n].T

            loop(0, nb, take, 8)

        loop(0, M, group)

    def weights(f):
        landed(f)
        flip(f)

    def weight(ref, f, j):
        return ref[f - 1, j // SB, lax.rem(j, SB) // nb, lax.rem(j, nb)]

    def side_weight(ref, f, j):
        at_j = ref.at[f - 1, j // SB, lax.rem(j, SB) // nb, lax.rem(j, nb)]
        rows = [at_j[pl.ds(pl.multiple_of(u * NBT + s0, nb), SB), :] for u in range(U)]
        return jnp.concatenate(rows, axis=0)

    def gradient(f, left, right):
        def one(n):
            a = jnp.concatenate([left(dc, n) for dc in range(C)], axis=1)
            b = jnp.concatenate([right(dc, n) for dc in range(C)], axis=1)
            gs[pl.ds(n, B, stride=GP), :] = dot_nt(a, b)

        loop(0, nb, one, 16)
        row = lax.broadcasted_iota(jnp.int32, (nb, B), 0)
        power = jnp.zeros((nb, B), jnp.int32)
        for n in range(nb):
            power = jnp.where(row == n, expo[f, n], power)
        scale = jnp.left_shift(jnp.ones_like(power), -power).astype(F32)
        inverse = jnp.left_shift(jnp.ones_like(power), 24 + power).astype(F32) * (2.0 ** -24)

        def quantize(g, slot):
            for s in range(CS):
                col = pl.ds(pl.multiple_of((g * CS + s) * B, B), B)
                total = gs[pl.ds(pl.multiple_of((g * CS + s) * GP, 8), nb), :] + e_v[f, :, col].astype(F32)
                code = jnp.clip(total * scale, -LIMIT, LIMIT)
                e_v[f, :, col] = (total - code * inverse).astype(BF16)
                cod[f, slot, :, s * B:(s + 1) * B] = code.astype(BF16)

        def away(step):
            d = lax.rem(step + 1, half_group)
            quantize(lax.rem(partner + 2 * d, G), d)
            q_copy(f, d).start()

        loop(0, half_group, away)
        loop(0, half_group, lambda d: quantize(lax.rem(dev + 2 * d, G), half_group + d))
        pltpu.make_async_copy(e_v.at[f], nerr.at[0, f], st.at[f]).start()
        return inverse

    def op_rows(k, dc, n):
        if dc:
            return ox[k, dc - 1, rows_at(n), :]
        if k < B4:
            return op[k, rows_at(c * nb + n), :]
        if k < D1:
            return block(COT if k == B4 else ONE, ma * nb + n)
        return od[k - D1, 0, rows_at(n), :]

    def ops(k):
        return functools.partial(op_rows, k)

    def spread_cot(dc):
        loop(0, nb, lambda i: scatter(i, c_v[half(dc), rows_at(i), :].astype(F32)), 8)
        pack(COT, dc)

    early, late = tuple(range(Q // Y)), tuple(range(Q // Y, Q))
    arrange()
    pl.semaphore_wait(barrier, M - 1 + G - 1)
    push(0)
    pair(0)
    for f in range(1, F):
        for dy in range(1, Y):
            y_copy(f, dy).start()
    for h in range(C):
        loads[h].wait()
    for dc in range(C - 1, -1, -1):
        spread_cot(dc)
        launch(COT, dc, early)
        near(COT, dc)

    forward(0, 1, 2)
    push(1)
    pair(1)
    forward(0, 2)
    push(2)
    push(3)
    pair(2)
    gather(0)
    weights_first()
    for h in range(C):
        loads[C + h].wait()
    for dc in range(C - 1, -1, -1):
        loop(0, nb, lambda i: scatter(i, dot(wt0[i], x_v[half(dc), rows_at(i), :])), 16)
        pack(ONE, dc)
        near(ONE, dc)
    for k, some in ((ONE, range(Q)), (COT, late)):
        for q in some:
            for dc in range(C - 1, -1, -1):
                launch(k, dc, (q,))
    forward(1, 1, 2)
    pair(3)
    forward(1, 2)
    forward(2, 1, 2)
    gather(1)
    forward(2, 2)
    weights(1)
    for q in early:
        arrive(COT, q)
    swap(B4)

    def first(q):
        arrive(ONE, q)
        base = chunk(q) * (NBT // Q)
        loop(0, NBT // Q, lambda n: stored(sf1, base + n, dot(weight(wt, 1, base + n), block(ONE, base + n))), 16)

    forward(3, 1, 2)
    gather(2)
    forward(3, 2)
    weights(2)
    for q in early:
        first(q)
    swap(M1)
    for q in late:
        first(q)

    def bent(i):
        v = gathered(sf1, i, PITCH, NBT).astype(BF16).astype(F32)
        square = v * v
        return v, square, jnp.tanh(C0 * (v + C1 * (square * v)))

    def middle(p, side):
        i = lax.rem(s0 + p, NBT)
        v, _, t = bent(i)
        hidden = (v * (0.5 * (1.0 + t))).astype(BF16)
        if side:
            op[HID, rows_at(p), :] = hidden
        stored(sf2, i, dot(weight(wt, 2, i), hidden))

    def slopes(i):
        v, square, t = bent(i)
        slope = 0.5 * (1.0 + t) + 0.5 * v * (1.0 - t * t) * (C0 * (1.0 + 3.0 * C1 * square))
        if tiled:
            stored(slp, i, slope)
        else:
            for u in range(U):
                sf1[pl.ds(u * NBT + i, NBT, stride=PITCH), :] = slope[u * NBT:(u + 1) * NBT]

    loop(0, SB, lambda p: middle(p, True), 8)
    swap(HID)
    loop(SB, NBT, lambda p: middle(p, False), 8)
    take_side(M2, sf2)
    swap(M2)
    gather(3)
    loop(0, NBT // 2, slopes, 8)
    loads[2 * C].wait()
    inverses = {}
    swapped(M2)
    swapped(B4)
    inverses[3] = gradient(3, ops(M2), ops(B4))
    loop(NBT // 2, NBT, slopes, 8)
    landed(3)

    def collect(k):
        for dc in range(C - 1, -1, -1):
            def one(n, dc=dc):
                value = gathered(sl, half(dc) * nb + n, SLP, SB)
                od[k - D1, dc, rows_at(n), :] = value.astype(BF16)

            loop(0, nb, one, 16)
            if dc:
                o_copy(k, dc).start()

    def fourth(p, side):
        j = lax.rem(s0 + p, NBT)
        two = taken(M2, sf2, p, j, side)
        sl[pl.ds(pl.multiple_of(j * SLP, 8), U * SB), :] = dot(side_weight(wt, 3, j), two)

    def last_forward(polls):
        if tiled:
            polls[0]()
        loop(0, SB, lambda p: fourth(p, True), 8)
        if tiled:
            polls[1]()
        loop(SB, NBT, lambda p: fourth(p, False), 8)
        if tiled:
            polls[2]()
        collect(LAST)

    if not tiled:
        flip(3)
        last_forward(())

    def third_back(q):
        base = chunk(q) * (NBT // Q)
        loop(0, NBT // Q, lambda n: stored(sb3, base + n, dot(weight(wn, 3, base + n), block(COT, base + n))), 16)

    for q in early:
        third_back(q)
    if tiled:
        flip(3)
    for q in late:
        arrive(COT, q)
        third_back(q)
    take_side(D3, sb3)
    swap(D3)

    def second_back(p, side):
        i = lax.rem(s0 + p, NBT)
        slope = slp[pl.ds(pl.multiple_of(i * PITCH, 8), B), :] if tiled else gathered(sf1, i, PITCH, NBT)
        stored(sb2, i, dot(weight(wn, 2, i), taken(D3, sb3, p, i, side)) * slope)

    loop(0, SB, lambda p: second_back(p, True), 8)
    combine(3)
    loop(SB, NBT, lambda p: second_back(p, False), 8)
    take_side(D2, sb2)
    swap(D2)
    swapped(HID)
    swapped(D3)
    inverses[2] = gradient(2, ops(HID), ops(D3))

    def first_back(p, side):
        j = lax.rem(s0 + p, NBT)
        sl[pl.ds(pl.multiple_of(j * SLP, 8), U * SB), :] = dot(side_weight(wn, 1, j), taken(D2, sb2, p, j, side))

    loop(0, SB, lambda p: first_back(p, True), 8)
    loop(SB, NBT, lambda p: first_back(p, False), 8)
    collect(D1)
    combine(2, 1, 2, False)
    swapped(M1)
    swapped(D2)
    inverses[1] = gradient(1, ops(M1), ops(D2))
    combine(2, 2)
    swapped(D1)
    inverses[0] = gradient(0, lambda dc, n: x_v[back(dc), rows_at(n), :], ops(D1))
    if tiled:
        last_forward((
            lambda: combine(1),
            lambda: combine(0, 1, 2, False),
            lambda: combine(0, 2, half_group - 1, False),
        ))
        combine(0, half_group - 1, None, False)
    else:
        combine(1)
    stores = []

    def save(ref, value_ref, h, sem):
        to = pl.ds(pl.multiple_of(h * LANES, LANES), LANES)
        stores.append(pltpu.make_async_copy(value_ref, ref.at[:, to], sem))
        stores[-1].start()

    for dc in range(C):
        def last_back(n, dc=dc):
            h = back(dc)
            value = c_v[h, rows_at(n), :].astype(F32) + dot(wn0[n], op_rows(D1, dc, n))
            c_v[h, rows_at(n), :] = value.astype(BF16)

        loop(0, nb, last_back, 8)
        save(igrad, c_v.at[back(dc)], back(dc), st.at[2 * F + dc])
    if tiled:
        combine(0, half_group)
    else:
        combine(0)

    def mean(f):
        loop(1, half_group, lambda d: c_copy(f, d).wait_recv())

        def column(s):
            col = pl.ds(pl.multiple_of(s * B, B), B)
            total = crx[f, 0, :, col].astype(F32)
            for g in range(1, half_group):
                total = total + crx[f, g, :, col].astype(F32)
            m_v[f, :, col] = total * inverses[f] / G

        loop(0, CS, column)
        stores.append(pltpu.make_async_copy(m_v.at[f], gmean.at[f], st.at[F + f]))
        stores[-1].start()

    swapped(LAST)
    for dc in range(C):
        ref = ox.at[LAST, dc - 1] if dc else od.at[LAST - D1, 0]

        def finish(n, dc=dc, ref=ref):
            value = x_v[back(dc), rows_at(n), :].astype(F32) + ref[rows_at(n), :].astype(F32)
            ref[rows_at(n), :] = value.astype(BF16)

        loop(0, nb, finish, 8)
        save(out, ref, back(dc), st.at[2 * F + C + dc])
    for f in (3, 2, 1, 0):
        mean(f)
    for f in range(F):
        pltpu.make_async_copy(e_v.at[f], nerr.at[0, f], st.at[f]).wait()
    for cp in stores:
        cp.wait()

    def handed(d):
        for f in range(F):
            if not line:
                w_copy(f, d).wait_send()
            q_copy(f, d).wait_send()
            c_copy(f, d).wait_send()
            p_copy(f, d, from_z(d)).wait_send()

    steps(1, half_group, handed)
    if line:
        for f in range(F):
            hop(f, dev, pair_z, 1, 1).wait_send()

        @pl.when(inner)
        def _():
            for f in range(F):
                hop(f, dev, 3 - z, 2, 2).wait_send()
                for copy in hops(f):
                    copy().wait_send()
    for f in range(F):
        p_copy(f, 0, dev).wait_send()
        q_copy(f, 0).wait_send()
    for f in range(1, F):
        for dy in range(1, Y):
            y_copy(f, dy).wait_send()
        for dc in range(1, C):
            loop(0, G, lambda n: k_copy(f, dc, n, dev).wait_send())
    for k in range(8):
        for dc in range(1, C):
            o_copy(k, dc).wait_send()
    for k in (COT, ONE):
        for dy in range(Y):
            for dc in range(C):
                if dy or dc:
                    for q in range(Q):
                        x_copy(k, dy, dc, q).wait_send()


def step(G, M, inp, cot, fac, expo, err):
    F, nb, S = fac.shape
    R, T = inp.shape
    C = T // LANES
    Y = M // C
    NBT = M * nb
    U = B // NBT
    SB = C * nb
    tiled = (S // B) % 16 == 0
    hbm = pl.BlockSpec(memory_space=pl.ANY)
    dma = pltpu.SemaphoreType.DMA
    return pl.pallas_call(
        functools.partial(kernel, G, M),
        out_shape=(
            jax.ShapeDtypeStruct((R, T), BF16),
            jax.ShapeDtypeStruct((R, T), BF16),
            jax.ShapeDtypeStruct(fac.shape, F32),
            jax.ShapeDtypeStruct(err.shape, BF16),
        ),
        in_specs=[hbm, hbm, hbm, pl.BlockSpec(memory_space=pltpu.SMEM), hbm],
        out_specs=(hbm,) * 4,
        scratch_shapes=[
            pltpu.VMEM((C, R, LANES), BF16),
            pltpu.VMEM((C, R, LANES), BF16),
            pltpu.VMEM((F, nb, B * B), BF16),
            pltpu.VMEM((max(NBT * (U * nb + PAD), B * (nb + PAD)), LANES), F32),
            pltpu.VMEM((2, C, NBT * U, nb, LANES), BF16),
            pltpu.VMEM((2, NBT * U, NBT, LANES), BF16),
            pltpu.VMEM((NBT * (B + PAD), LANES), F32),
            pltpu.VMEM((NBT * (B + PAD), LANES), F32),
            pltpu.VMEM((NBT * (B + PAD), LANES), F32),
            pltpu.VMEM((NBT * (B + PAD) if tiled else B, LANES), F32),
            pltpu.VMEM((NBT * (U * SB + PAD), LANES), F32),
            pltpu.VMEM((4, SB * B, LANES), BF16),
            pltpu.VMEM((8, C - 1, R, LANES), BF16),
            pltpu.VMEM((2, C, R, LANES), BF16),
            pltpu.VMEM((F, nb, S), BF16),
            pltpu.VMEM((1, nb, S) if tiled else (G, nb, S), BF16),
            pltpu.VMEM((1, 1, 1, 1, nb, S) if tiled else (F - 1, G, C, Y, nb, S), BF16),
            pltpu.VMEM((nb, B, B), BF16),
            pltpu.VMEM((nb, B, B), BF16),
            pltpu.VMEM((F - 1, Y, C, nb, B, B), BF16),
            pltpu.VMEM((F - 1, Y, C, nb, B, B), BF16),
            pltpu.VMEM((F, G, nb, S), BF16),
            pltpu.VMEM((F, G, nb, S), BF16),
            pltpu.VMEM((F, nb, S), F32),
            dma((2 * C + 1 + F,)),
            dma((2 * F + 2 * C,)),
            dma((2, M, Q)),
            dma((2, M, Q)),
            dma((F, Y)),
            dma((F, Y)),
            dma((F, max(G // 2, 6))),
            dma((F, G // 2)),
            dma((F, G // 2)),
            dma((F, G // 2)),
            dma((F, C, G)),
            dma((F, C, G)),
            dma((8, C)),
            dma((8, C)),
            dma((F, G // 2)),
            dma((F, G // 2)),
            dma((F, G // 2)),
            dma((F, G // 2)),
        ],
        compiler_params=pltpu.CompilerParams(
            collective_id=0, has_side_effects=True, vmem_limit_bytes=62 * 1024 * 1024
        ),
    )(inp, cot, fac, expo, err)


def solution(mesh):
    G, M = mesh.shape["dev"], mesh.shape["ma"]
    in_specs = (
        P("ma", "dev"),
        P("ma", "dev"),
        P(None, "ma", "dev"),
        P(None, "ma"),
        P("dev", None, "ma", None),
    )
    out_specs = (P("ma", "dev"), P("ma", "dev"), P(None, "ma", "dev"), P("dev", None, "ma", None))
    return jax.shard_map(
        functools.partial(step, G, M), mesh=mesh, in_specs=in_specs, out_specs=out_specs, check_vma=False
    )
```
